512 devices in a mesh: phi: 64 (over y, x, z_hi, core), row: 8 (over z_lo).
Axes of the slice: x: 4, y: 4, z: 16 (z_hi: 2, z_lo: 8; z = z_hi * 8 + z_lo), core: 2. Of those that a mesh axis runs over, the one named last changes fastest.
Arguments:
- magnetogram: bfloat16 [16384, 1024], P('phi', 'row'), may hold values from -6 to 6
- col_owner: int32 [16384], P('phi'), may hold values from 0 to 63, as said below
- col_offset: int32 [16384], P('phi'), may hold values from 0 to 7, as said below
- phi_weight: bfloat16 [512, 3072], P(None, 'phi'), may hold values from -0.375 to 0.375
- theta_weight: bfloat16 [1024, 128], P('row'), may hold values from -0.1875 to 0.1875
- radial_coef: float32 [32], replicated, may hold values from 0.3 to 3
- theta_coef: float32 [128], replicated, may hold values from 0.3 to 3
- phi_coef: float32 [3072], replicated, may hold values from 0.3 to 3
- start_field: float32 [32, 3072, 128], P('row', 'phi'), may hold values from -0.3125 to 0.3125
Outputs:
- solution_field: float32 [32, 3072, 128], P('row', 'phi')
- residual: float32 [32, 3072, 128], P('row', 'phi')
The draws below stay inside these ranges and needn't reach their ends.
Inputs may be any that keep to these rules, and one draw needn't show every extreme that they name: `col_owner`: within each aligned block of 256 columns (the columns of one index of phi) at most 8 columns share an owner, and one owner receives exactly 8 columns from every block. `col_offset`: columns of one aligned block of 256 columns that share an owner have distinct offsets.
All inputs are finite; a program needn't handle non-finite values.
Results may differ from the reference program's by a relative error of at most 0.019.
Values may be sent and summed in bfloat16 or wider, within the bound.
A program may use at most 64 MiB of HBM per device.

```python
import math
import jax
import jax.numpy as jnp
from jax import lax

CP = 48
NT = 128
MCOL_DEV = 256
ITERS = 2
NR = 32
NP = 3072
MT = 1024
MAGC = 16384
SLOTS = 512
CAP = 8


def slot_table(key):
    sources = MAGC // MCOL_DEV
    base = jax.random.fold_in(key, 7)
    hot = jax.random.randint(jax.random.fold_in(base, 1), (), 0, sources)

    def one_source(source):
        source_key = jax.random.fold_in(base, source + 11)
        others = jax.random.permutation(jax.random.fold_in(source_key, 1), SLOTS - CAP)[:MCOL_DEV - CAP]
        others = jnp.where(others >= hot * CAP, others + CAP, others)
        hots = hot * CAP + jnp.arange(CAP, dtype=jnp.int32)
        chosen = jnp.concatenate([hots, others.astype(jnp.int32)])
        return jax.random.permutation(jax.random.fold_in(source_key, 2), chosen)
    return jax.vmap(one_source)(jnp.arange(sources, dtype=jnp.int32)).reshape(-1).astype(jnp.int32)


def draw_col_owner(key, part):
    return (slot_table(key) // CAP).astype(jnp.int32)


def draw_col_offset(key, part):
    return (slot_table(key) % CAP).astype(jnp.int32)


def draw_start_field(key, part):
    radial_ramp = 1.0 + 2.0 * jnp.arange(NR, dtype=jnp.float32) / max(NR - 1, 1)
    phi_ramp = 1.0 + 2.0 * jnp.arange(NP, dtype=jnp.float32) / max(NP - 1, 1)
    rough = jnp.clip(jax.random.normal(key, (NR, NP, NT), jnp.float32), -4.0, 4.0)
    return (0.005 * rough * radial_ramp[:, None, None] * phi_ramp[None, :, None]).astype(jnp.float32)


def block_levels(rng, dims, shards, smallest, top_value):
    gain = 1.0
    for dim, parts in shards:
        draws = jax.random.uniform(jax.random.fold_in(jax.random.fold_in(rng, 6), dim), (parts,), jnp.float32, smallest / len(shards), top_value / len(shards))
        gain = gain * jnp.repeat(jnp.exp(draws), dims[dim] // parts).reshape((-1,) + (1,) * (len(dims) - 1 - dim))
    return gain


def centred(own_key, dims, spread, most, shards=(), kind=jnp.bfloat16):
    array = spread * jax.random.normal(own_key, dims, jnp.float32)
    if shards:
        array = array * block_levels(own_key, dims, shards, -0.22, 0.18)
    return jnp.clip(array, -most, most).astype(kind)


def setup_inputs(seed: int = 0) -> dict:
    key_list = jax.random.split(jax.random.key(seed), 10)
    magnetogram = centred(key_list[0], (MAGC, MT), 1.0, 6.0, ((0, 64), (1, 8)))
    col_owner = draw_col_owner(jax.random.fold_in(key_list[9], 71), 0)
    col_offset = draw_col_offset(jax.random.fold_in(key_list[9], 71), 0)
    phi_weight = centred(key_list[3], (SLOTS, NP), MCOL_DEV ** -0.5, 0.375, ((1, 64),))
    theta_weight = centred(key_list[4], (MT, NT), MT ** -0.5, 0.1875, ((0, 8),))
    radial_coef = jnp.clip(jnp.exp(jax.random.uniform(key_list[5], (NR,), jnp.float32, math.log(0.3), math.log(3.0))), 0.3, 3.0)
    theta_coef = jnp.clip(jnp.exp(jax.random.uniform(key_list[6], (NT,), jnp.float32, math.log(0.3), math.log(3.0))), 0.3, 3.0)
    phi_coef = jnp.clip(jnp.exp(jax.random.uniform(key_list[7], (NP,), jnp.float32, math.log(0.3), math.log(3.0))), 0.3, 3.0)
    start_field = draw_start_field(jax.random.fold_in(key_list[9], 71), 0)
    return {"magnetogram": magnetogram, "col_owner": col_owner, "col_offset": col_offset, "phi_weight": phi_weight, "theta_weight": theta_weight, "radial_coef": radial_coef, "theta_coef": theta_coef, "phi_coef": phi_coef, "start_field": start_field}


def face_coefs(radial_coef, theta_coef, phi_coef):
    radial_mid = 0.5 * (radial_coef[:-1] + radial_coef[1:])
    radial_upper = jnp.concatenate([radial_mid, radial_coef[-1:]])
    radial_lower = jnp.concatenate([radial_coef[:1], radial_mid])
    theta_mid = 0.5 * (theta_coef[:-1] + theta_coef[1:])
    zero_one = jnp.zeros((1,), jnp.float32)
    theta_upper = jnp.concatenate([theta_mid, zero_one])
    theta_lower = jnp.concatenate([zero_one, theta_mid])
    phi_upper = 0.5 * (phi_coef + jnp.roll(phi_coef, -1))
    phi_lower = jnp.roll(phi_upper, 1)
    return radial_upper, radial_lower, theta_upper, theta_lower, phi_upper, phi_lower


def apply_operator(field, coefs):
    radial_upper, radial_lower, theta_upper, theta_lower, phi_upper, phi_lower = coefs
    radial_pad = jnp.pad(field, ((1, 1), (0, 0), (0, 0)))
    theta_pad = jnp.pad(field, ((0, 0), (0, 0), (1, 1)))
    phi_next = jnp.roll(field, -1, axis=1)
    phi_prev = jnp.roll(field, 1, axis=1)
    result = radial_upper[:, None, None] * (field - radial_pad[2:])
    result = result + radial_lower[:, None, None] * (field - radial_pad[:-2])
    result = result + theta_upper[None, None, :] * (field - theta_pad[:, :, 2:])
    result = result + theta_lower[None, None, :] * (field - theta_pad[:, :, :-2])
    result = result + phi_upper[None, :, None] * (field - phi_next)
    result = result + phi_lower[None, :, None] * (field - phi_prev)
    return result


def reference(magnetogram, col_owner, col_offset, phi_weight, theta_weight, radial_coef, theta_coef, phi_coef, start_field):
    columns = jnp.dot(magnetogram, theta_weight, preferred_element_type=jnp.float32)
    sources = MAGC // MCOL_DEV
    slot_index = ((jnp.arange(MAGC, dtype=jnp.int32) // MCOL_DEV) * CAP + col_offset).astype(jnp.int32)

    def add_block(total, block_index):
        start = (block_index * MCOL_DEV).astype(jnp.int32)
        block_cols = lax.dynamic_slice_in_dim(columns, start, MCOL_DEV, 0)
        owners = lax.dynamic_slice_in_dim(col_owner, start, MCOL_DEV, 0).astype(jnp.int32)
        slots = lax.dynamic_slice_in_dim(slot_index, start, MCOL_DEV, 0).astype(jnp.int32)
        weight_rows = phi_weight[slots].reshape(MCOL_DEV, sources, CP)
        chosen = jnp.take_along_axis(weight_rows, owners[:, None, None], axis=1)[:, 0, :].astype(jnp.float32)
        contrib = chosen[:, :, None] * block_cols[:, None, :]
        return total + jax.ops.segment_sum(contrib, owners, num_segments=sources), None

    init = jnp.zeros((sources, CP, NT), jnp.float32)
    total, unused = lax.scan(add_block, init, jnp.arange(sources, dtype=jnp.int32))
    boundary = total.reshape(NP, NT)
    coefs = face_coefs(radial_coef, theta_coef, phi_coef)
    diag = (coefs[0][:, None, None] + coefs[1][:, None, None] + coefs[2][None, None, :]
            + coefs[3][None, None, :] + coefs[4][None, :, None] + coefs[5][None, :, None])
    inv_diag = 1.0 / diag
    right_side = jnp.concatenate([(coefs[1][0] * boundary)[None], jnp.zeros((NR - 1, NP, NT), jnp.float32)], axis=0)
    solution_field = start_field
    residual = right_side - apply_operator(start_field, coefs)
    precond = residual * inv_diag
    direction = precond
    norm_now = jnp.sum(residual * precond)
    for sweep_index in range(ITERS):
        image = apply_operator(direction, coefs)
        alpha = norm_now / jnp.sum(direction * image)
        solution_field = solution_field + alpha * direction
        residual = residual - alpha * image
        if sweep_index + 1 < ITERS:
            precond = residual * inv_diag
            norm_next = jnp.sum(residual * precond)
            direction = precond + (norm_next / norm_now) * direction
            norm_now = norm_next
    return solution_field, residual
```

```python
import functools

import jax
import jax.numpy as jnp
from jax import lax
from jax.experimental import pallas as pl
from jax.experimental.pallas import tpu as pltpu
from jax.sharding import PartitionSpec as P

MESH = pl.DeviceIdType.MESH
CAP = 8
PAD = 8
F32 = jnp.float32
BF16 = jnp.bfloat16
NT_DIMS = (((1,), (1,)), ((), ()))


def roll(x, shift, axis):
    return pltpu.roll(x, shift % x.shape[axis], axis)


def kernel(
    phis,
    rows,
    mag_ref,
    owner_ref,
    offset_ref,
    weight_ref,
    theta_ref,
    radial_ref,
    theta_coef_ref,
    phi_coef_ref,
    start_ref,
    x_out,
    r_out,
    pack,
    recv,
    wsend,
    wrecv,
    part,
    main,
    low,
    high,
    bound,
    field,
    inverse,
    base,
    sums,
    sums_plane,
    sums_column,
    pack_send,
    pack_recv,
    w_send,
    w_recv,
    part_send,
    main_recv,
    low_recv,
    high_recv,
    field_send,
    field_recv,
    plane_send,
    plane_recv,
    column_send,
    column_recv,
):
    phi = lax.axis_index("phi")
    row = lax.axis_index("row")
    planes = phis // 2
    column = 2 * rows
    cells = start_ref.shape[1]
    layers = start_ref.shape[0]
    width = start_ref.shape[2]
    half = lax.rem(lax.div(phi, 2), 2)
    other = 1 - half
    here = lax.div(phi, 4) * 2 + lax.rem(phi, 2)
    depth = half * rows + row
    slots = planes * 2 * CAP

    def phi_of(place, side):
        return lax.div(place, 2) * 4 + side * 2 + lax.rem(place, 2)

    partner = phi_of(here, other)

    def wrap(index):
        return lax.rem(index + phis, phis)

    up_phi = wrap(phi + 1)
    down_phi = wrap(phi - 1)

    barrier = pltpu.get_barrier_semaphore()

    def greet(device, level):
        pl.semaphore_signal(barrier, inc=1, device_id=(device, level), device_id_type=MESH)

    @pl.when(row == 0)
    def _():
        @pl.loop(0, column)
        def _(z):
            side, level = lax.div(z, rows), lax.rem(z, rows)
            for owner in (down_phi, up_phi):
                place = lax.div(owner, 4) * 2 + lax.rem(owner, 2)
                greet(phi_of(place, side), level)

    @pl.loop(0, column)
    def _(z):
        @pl.when(z != depth)
        def _():
            greet(phi_of(here, lax.div(z, rows)), lax.rem(z, rows))

    @pl.loop(0, planes)
    def _(place):
        @pl.when(place != here)
        def _():
            greet(phi_of(place, half), row)

    for near in (down_phi, up_phi):
        greet(near, row)

        @pl.when(row > 0)
        def _():
            greet(near, row - 1)

        @pl.when(row < rows - 1)
        def _():
            greet(near, row + 1)

    owner = owner_ref[...]
    target = (owner >> 2) * 32 + (owner & 1) * 16 + ((owner >> 1) & 1) * 8 + offset_ref[...]
    slot = lax.broadcasted_iota(jnp.int32, (slots, owner.shape[1]), 0)
    chosen = jnp.where(slot == target, 1.0, 0.0).astype(BF16)
    packed = jnp.dot(chosen, mag_ref[...], preferred_element_type=F32).astype(BF16)
    pack[...] = packed.reshape(planes, 2 * CAP, width)
    recv[here] = pack[here]

    weights = weight_ref[...]
    from_slot = lax.broadcasted_iota(jnp.int32, (slots, planes * CAP), 0)
    to_slot = lax.broadcasted_iota(jnp.int32, (slots, planes * CAP), 1)
    source = to_slot >> 3
    natural = ((source >> 1) * 4 + other * 2 + (source & 1)) * CAP + (to_slot & 7)
    pick = jnp.where(from_slot == natural, 1.0, 0.0).astype(BF16)
    wsend[...] = jnp.dot(weights, pick, preferred_element_type=F32).astype(BF16)

    for layer in range(layers):
        field[3 + layer, PAD : PAD + cells, :] = start_ref[layer]

    @pl.when(row == 0)
    def _():
        field[0:3] = jnp.zeros((3,) + field.shape[1:], F32)

    @pl.when(row == rows - 1)
    def _():
        field[3 + layers : 6 + layers] = jnp.zeros((3,) + field.shape[1:], F32)

    pl.semaphore_wait(
        barrier,
        (planes - 1)
        + (column - 1)
        + 4
        + 2
        * (
            1
            + jnp.where(row > 0, 1, 0).astype(jnp.int32)
            + jnp.where(row < rows - 1, 1, 0).astype(jnp.int32)
        ),
    )

    def remote(src, dst, send, receive, device, level):
        return pltpu.make_async_remote_copy(
            src_ref=src,
            dst_ref=dst,
            send_sem=send,
            recv_sem=receive,
            device_id=(device, level),
            device_id_type=MESH,
        )

    weight_copy = remote(
        wsend, wrecv, w_send, w_recv, partner, lax.rem(row + rows // 2, rows)
    )
    weight_copy.start()

    def pack_copy(place):
        return remote(
            pack.at[place],
            recv.at[here],
            pack_send.at[place],
            pack_recv.at[here],
            phi_of(place, half),
            row,
        )

    @pl.loop(0, planes)
    def _(place):
        @pl.when(place != here)
        def _():
            pack_copy(place).start()

    top, bottom = slice(layers - 3, layers), slice(0, 3)
    ghosts = []
    for side_index, (near, source_cells, ghost_cells) in enumerate(
        (
            (up_phi, slice(cells - PAD, cells), slice(0, PAD)),
            (down_phi, slice(0, PAD), slice(PAD + cells, 2 * PAD + cells)),
        )
    ):
        for kind, (step, source_layers, ghost_layers) in enumerate(
            (
                (0, slice(0, layers), slice(3, 3 + layers)),
                (1, slice(layers - 2, layers), slice(1, 3)),
                (-1, slice(0, 2), slice(3 + layers, 5 + layers)),
            )
        ):
            ghosts.append(
                (side_index * 3 + kind, near, step, source_layers, source_cells, ghost_layers, ghost_cells)
            )
    middle = slice(PAD, PAD + cells)
    ghosts.append((6, phi, 1, top, slice(0, cells), slice(0, 3), middle))
    ghosts.append((7, phi, -1, bottom, slice(0, cells), slice(3 + layers, 6 + layers), middle))

    def each_ghost(act, sending):
        for index, near, step, source_layers, source_cells, ghost_layers, ghost_cells in ghosts:
            copy = remote(
                start_ref.at[source_layers, source_cells],
                field.at[ghost_layers, ghost_cells],
                field_send.at[index],
                field_recv.at[index],
                near,
                row + step,
            )
            if step == 0:
                act(copy)
            else:
                exists = row < rows - 1 if (step > 0) == sending else row > 0

                @pl.when(exists)
                def _():
                    act(copy)

    each_ghost(lambda copy: copy.start(), True)

    tall = cells + 2 * PAD
    lanes = lax.broadcasted_iota(jnp.int32, (tall, width), 1)
    theta_coef = jnp.broadcast_to(theta_coef_ref[...], (tall, width))
    theta_upper = jnp.where(lanes < width - 1, 0.5 * (theta_coef + roll(theta_coef, -1, 1)), 0.0)
    theta_lower = jnp.where(lanes > 0, roll(theta_upper, 1, 1), 0.0)
    lines = phi_coef_ref.shape[0]
    first = lax.rem(phi * cells - PAD + lines * width, lines * width)
    line = lax.div(first, width)
    shift = width - lax.rem(first, width)
    near_line = phi_coef_ref[pl.ds(line, 1), :]
    next_line = phi_coef_ref[pl.ds(lax.rem(line + 1, lines), 1), :]
    lane8 = lax.broadcasted_iota(jnp.int32, (8, width), 1)
    window = jnp.where(
        lane8 < shift,
        pltpu.roll(jnp.broadcast_to(near_line, (8, width)), shift, 1),
        pltpu.roll(jnp.broadcast_to(next_line, (8, width)), shift, 1),
    )
    phi_face = 0.5 * (window + roll(window, -1, 1))
    phi_face = jnp.broadcast_to(phi_face[0:1], (width, width)).T
    phi_upper = phi_face[:tall]
    phi_lower = roll(phi_upper, 1, 0)
    top_index = layers * rows - 1

    def coef_at(index):
        return radial_ref[jnp.clip(index, 0, top_index)]

    radial_lower = [
        0.5 * (coef_at(row * layers + i - 4) + coef_at(row * layers + i - 3))
        for i in range(layers + 7)
    ]
    radial_upper = radial_lower[1:]
    around = phi_upper + phi_lower + theta_upper + theta_lower
    for i in range(1, layers + 5):
        index = row * layers + i - 3
        inside = jnp.where(jnp.logical_and(index >= 0, index <= top_index), 1.0, 0.0).astype(F32)
        inverse[i] = inside / (radial_upper[i] + radial_lower[i] + around)

    def image(values, i):
        value = values[i]
        result = radial_upper[i] * (value - values[i + 1])
        result = result + radial_lower[i] * (value - values[i - 1])
        result = result + theta_upper * (value - roll(value, -1, 1))
        result = result + theta_lower * (value - roll(value, 1, 1))
        result = result + phi_upper * (value - roll(value, -1, 0))
        return result + phi_lower * (value - roll(value, 1, 0))

    wide = (slots, slots)
    from_slot = lax.broadcasted_iota(jnp.int32, wide, 0)
    to_slot = lax.broadcasted_iota(jnp.int32, wide, 1)
    source = to_slot >> 4
    natural = ((source >> 1) * 4 + half * 2 + (source & 1)) * CAP + (to_slot & 7)
    mine = jnp.logical_and(from_slot == natural, ((to_slot >> 3) & 1) == half)
    own_weights = jnp.dot(
        weights, jnp.where(mine, 1.0, 0.0).astype(BF16), preferred_element_type=F32
    ).astype(BF16)
    from_slot = lax.broadcasted_iota(jnp.int32, (planes * CAP, slots), 0)
    to_slot = lax.broadcasted_iota(jnp.int32, (planes * CAP, slots), 1)
    theirs = jnp.logical_and(
        from_slot == (to_slot >> 4) * CAP + (to_slot & 7), ((to_slot >> 3) & 1) == other
    )
    theirs = jnp.where(theirs, 1.0, 0.0).astype(BF16)
    weight_copy.wait_recv()
    partner_weights = jnp.dot(wrecv[...], theirs, preferred_element_type=F32).astype(BF16)
    both_weights = jnp.concatenate([own_weights, partner_weights], axis=0)

    def pack_arrival(place):
        return remote(
            pack.at[place],
            recv.at[place],
            pack_send.at[place],
            pack_recv.at[place],
            phi_of(place, half),
            row,
        )

    @pl.loop(0, planes)
    def _(place):
        @pl.when(place != here)
        def _():
            pack_arrival(place).wait_recv()

    columns = jnp.dot(
        both_weights, recv[...].reshape(slots, width), preferred_element_type=F32
    )
    part[...] = jnp.dot(
        columns,
        theta_ref[...].astype(F32),
        preferred_element_type=F32,
        precision=lax.Precision.HIGHEST,
    )

    def part_copies():
        copies = []
        for index, owner in enumerate((phi, partner)):
            start = index * cells
            copies.append(
                remote(
                    part.at[start : start + PAD],
                    high.at[depth],
                    part_send.at[3 * index],
                    high_recv.at[depth],
                    wrap(owner - 1),
                    0,
                )
            )
            copies.append(
                remote(
                    part.at[start + cells - PAD : start + cells],
                    low.at[depth],
                    part_send.at[3 * index + 1],
                    low_recv.at[depth],
                    wrap(owner + 1),
                    0,
                )
            )
            copies.append(
                remote(
                    part.at[start : start + cells],
                    main.at[depth],
                    part_send.at[3 * index + 2],
                    main_recv.at[depth],
                    owner,
                    0,
                )
            )
        return copies

    part_list = part_copies()
    for index in (5, 3, 4, 0, 1):
        part_list[index].start()

    @pl.when(row > 0)
    def _():
        part_list[2].start()

    each_ghost(lambda copy: copy.wait_recv(), False)
    values = [field[i] for i in range(layers + 6)]
    for i in range(1, layers + 5):
        base[i] = -image(values, i)

    @pl.when(row == 0)
    def _():
        main[depth] = part[0:cells]

        @pl.loop(0, column)
        def _(z):
            def arrival(src, buffer, semaphore):
                return remote(
                    src, buffer.at[z], part_send.at[0], semaphore.at[z], phi, 0
                )

            arrival(part.at[0:PAD], low, low_recv).wait_recv()
            arrival(part.at[0:PAD], high, high_recv).wait_recv()

            @pl.when(z != depth)
            def _():
                arrival(part.at[0:cells], main, main_recv).wait_recv()

        bound[0:PAD] = jnp.sum(low[...], axis=0)
        bound[PAD : PAD + cells] = jnp.sum(main[...], axis=0)
        bound[PAD + cells :] = jnp.sum(high[...], axis=0)
        base[3] = base[3] + radial_lower[3] * bound[...]

    residual = {i: base[i] for i in range(1, layers + 5)}
    precond = {i: residual[i] * inverse[i] for i in range(1, layers + 5)}
    first_image = {i: image(precond, i) for i in range(2, layers + 4)}
    scaled = {i: first_image[i] * inverse[i] for i in range(2, layers + 4)}
    second_image = {i: image(scaled, i) for i in range(3, layers + 3)}

    def inner(left, right):
        total = 0.0
        for i in range(3, layers + 3):
            product = left[i] * right[i]
            for k in range(PAD, PAD + cells, 8):
                total = total + product[k : k + 8]
        return jnp.sum(jnp.sum(total, axis=0, keepdims=True), axis=1, keepdims=True)

    lane = lax.broadcasted_iota(jnp.int32, (1, width), 1)
    four = (
        inner(residual, precond),
        inner(precond, first_image),
        inner(first_image, scaled),
        inner(scaled, second_image),
    )
    packed_sums = jnp.zeros((1, width), F32)
    for index, value in enumerate(four):
        packed_sums = jnp.where(lane == index, value, packed_sums)
    sums[0] = packed_sums
    sums_plane[here] = packed_sums

    def plane_copy(place, slot):
        return remote(
            sums.at[0],
            sums_plane.at[slot],
            plane_send.at[place],
            plane_recv.at[slot],
            phi_of(place, half),
            row,
        )

    @pl.loop(0, planes)
    def _(place):
        @pl.when(place != here)
        def _():
            plane_copy(place, here).start()

    @pl.loop(0, planes)
    def _(place):
        @pl.when(place != here)
        def _():
            plane_copy(place, place).wait_recv()

    plane_sum = jnp.sum(sums_plane[...], axis=0)
    sums[1] = plane_sum
    sums_column[depth] = plane_sum

    def column_copy(z, slot):
        return remote(
            sums.at[1],
            sums_column.at[slot],
            column_send.at[z],
            column_recv.at[slot],
            phi_of(here, lax.div(z, rows)),
            lax.rem(z, rows),
        )

    @pl.loop(0, column)
    def _(z):
        @pl.when(z != depth)
        def _():
            column_copy(z, depth).start()

    @pl.loop(0, column)
    def _(z):
        @pl.when(z != depth)
        def _():
            column_copy(z, z).wait_recv()

    totals = jnp.sum(sums_column[...], axis=0)
    rz, pq, qw, wt = (
        jnp.sum(jnp.where(lane == index, totals, 0.0), axis=1, keepdims=True)
        for index in range(4)
    )
    step0 = rz / pq
    rz_next = step0 * step0 * qw - rz
    ratio = 1.0 + rz_next / rz
    step1 = rz_next / (step0 * step0 * wt - ratio * ratio * pq)
    along = step0 + step1 * ratio
    across = step0 * step1
    for layer in range(layers):
        i = 3 + layer
        part_of = slice(PAD, PAD + cells)
        x_out[layer] = (
            start_ref[layer] + along * precond[i][part_of] - across * scaled[i][part_of]
        )
        r_out[layer] = (
            residual[i][part_of]
            - along * first_image[i][part_of]
            + across * second_image[i][part_of]
        )

    weight_copy.wait_send()

    @pl.loop(0, planes)
    def _(place):
        @pl.when(place != here)
        def _():
            pack_copy(place).wait_send()
            plane_copy(place, here).wait_send()

    @pl.loop(0, column)
    def _(z):
        @pl.when(z != depth)
        def _():
            column_copy(z, depth).wait_send()

    each_ghost(lambda copy: copy.wait_send(), True)
    for index in (5, 3, 4, 0, 1):
        part_list[index].wait_send()

    @pl.when(row > 0)
    def _():
        part_list[2].wait_send()


def body(
    magnetogram,
    col_owner,
    col_offset,
    phi_weight,
    theta_weight,
    radial_coef,
    theta_coef,
    phi_coef,
    start_field,
):
    phis, rows = lax.axis_size("phi"), lax.axis_size("row")
    layers, cells, width = start_field.shape
    planes, column = phis // 2, 2 * rows
    slots = phis * CAP
    tall = cells + 2 * PAD
    dma = pltpu.SemaphoreType.DMA
    vmem = pl.BlockSpec(memory_space=pltpu.VMEM)
    in_specs = [vmem] * 9
    in_specs[5] = pl.BlockSpec(memory_space=pltpu.SMEM)
    shape = jax.ShapeDtypeStruct(start_field.shape, F32)
    return pl.pallas_call(
        functools.partial(kernel, phis, rows),
        out_shape=(shape, shape),
        in_specs=in_specs,
        out_specs=(vmem, vmem),
        scratch_shapes=[
            pltpu.VMEM((planes, 2 * CAP, width), BF16),
            pltpu.VMEM((planes, 2 * CAP, width), BF16),
            pltpu.VMEM((cells, planes * CAP), BF16),
            pltpu.VMEM((cells, planes * CAP), BF16),
            pltpu.VMEM((2 * cells, width), F32),
            pltpu.VMEM((column, cells, width), F32),
            pltpu.VMEM((column, PAD, width), F32),
            pltpu.VMEM((column, PAD, width), F32),
            pltpu.VMEM((tall, width), F32),
            pltpu.VMEM((layers + 6, tall, width), F32),
            pltpu.VMEM((layers + 6, tall, width), F32),
            pltpu.VMEM((layers + 6, tall, width), F32),
            pltpu.VMEM((2, 1, width), F32),
            pltpu.VMEM((planes, 1, width), F32),
            pltpu.VMEM((column, 1, width), F32),
            dma((planes,)),
            dma((planes,)),
            dma,
            dma,
            dma((6,)),
            dma((column,)),
            dma((column,)),
            dma((column,)),
            dma((8,)),
            dma((8,)),
            dma((planes,)),
            dma((planes,)),
            dma((column,)),
            dma((column,)),
        ],
        compiler_params=pltpu.CompilerParams(collective_id=0, has_side_effects=True),
    )(
        magnetogram,
        col_owner.reshape(1, -1),
        col_offset.reshape(1, -1),
        phi_weight.T,
        theta_weight,
        radial_coef,
        theta_coef.reshape(1, -1),
        phi_coef.reshape(-1, width),
        start_field,
    )


def solution(mesh):
    in_specs = (
        P("phi", "row"),
        P("phi"),
        P("phi"),
        P(None, "phi"),
        P("row", None),
        P(),
        P(),
        P(),
        P("row", "phi", None),
    )
    out_specs = (P("row", "phi", None), P("row", "phi", None))
    return jax.shard_map(body, mesh=mesh, in_specs=in_specs, out_specs=out_specs, check_vma=False)
```

```python
import functools

import jax
import jax.numpy as jnp
from jax import lax
from jax.experimental import pallas as pl
from jax.experimental.pallas import tpu as pltpu
from jax.sharding import PartitionSpec as P

MESH = pl.DeviceIdType.MESH
CAP = 8
PAD = 8
EDGE = 3
F32 = jnp.float32
BF16 = jnp.bfloat16


def roll(x, shift, axis):
    return pltpu.roll(x, shift % x.shape[axis], axis)


def kernel(
    phis,
    rows,
    mag_hbm,
    owner_hbm,
    offset_hbm,
    weight_hbm,
    theta_hbm,
    radial_hbm,
    theta_coef_hbm,
    phi_coef_hbm,
    start_hbm,
    fields_out,
    coef_out,
    mag_ref,
    owner_ref,
    offset_ref,
    weight_ref,
    theta_ref,
    radial_ref,
    theta_coef_ref,
    phi_coef_ref,
    pack,
    recv,
    wsend,
    wrecv,
    part,
    main,
    near_part,
    far_part,
    bound,
    forward,
    far_forward,
    mid,
    near_ghost,
    far_ghost,
    shadow_mid,
    shadow_near,
    field,
    inverse,
    faces,
    values,
    sums,
    sums_column,
    sums_plane,
    totals,
    in_sem,
    out_sem,
    pack_send,
    pack_recv,
    w_send,
    w_recv,
    part_send,
    main_recv,
    near_recv,
    far_recv,
    forward_send,
    forward_recv,
    radial_send,
    radial_recv,
    nghost_send,
    nghost_recv,
    fghost_send,
    fghost_recv,
    shadow_send,
    shadow_recv,
    column_send,
    column_recv,
    plane_send,
    plane_recv,
    total_send,
    total_recv,
):
    phi = lax.axis_index("phi")
    row = lax.axis_index("row")
    planes = phis // 2
    column = 2 * rows
    layers = start_hbm.shape[0]
    cells = start_hbm.shape[1]
    width = start_hbm.shape[2]
    tall = cells + 2 * PAD
    deep = layers + 2 * EDGE
    core = lax.rem(phi, 2)
    half = lax.rem(lax.div(phi, 2), 2)
    other = 1 - half
    here = lax.div(phi, 4) * 2 + core
    depth = half * rows + row
    slots = planes * 2 * CAP
    is_root = depth == 0
    is_second = depth == rows

    def phi_of(place, side):
        return lax.div(place, 2) * 4 + side * 2 + lax.rem(place, 2)

    def wrap(index):
        return lax.rem(index + phis, phis)

    def place_of(index):
        return lax.div(index, 4) * 2 + lax.rem(index, 2)

    twin = here + 1 - 2 * core
    near = phi + 1 - 2 * core
    far_step = 2 * core - 1
    far = wrap(phi + far_step)
    early_phi, late_phi = phi_of(here, 0), phi_of(here, 1)
    far_of_early, far_of_late = wrap(early_phi + far_step), wrap(late_phi + far_step)
    early_twin_phi = phi_of(twin, 0)
    last = cells - PAD
    near_src = pl.multiple_of((1 - core) * last, PAD)
    far_src = pl.multiple_of(core * last, PAD)

    inputs = [
        pltpu.make_async_copy(src, dst, in_sem.at[index])
        for index, (src, dst) in enumerate(
            (
                (owner_hbm, owner_ref),
                (offset_hbm, offset_ref),
                (mag_hbm, mag_ref),
                (weight_hbm, weight_ref),
                (start_hbm, mid.at[EDGE : EDGE + layers]),
                (radial_hbm, radial_ref),
                (theta_coef_hbm, theta_coef_ref),
                (phi_coef_hbm, phi_coef_ref),
                (theta_hbm, theta_ref),
            )
        )
    ]
    for copy in inputs:
        copy.start()

    has_next = row < rows - 1
    has_previous = row > 0

    def steps(act):
        act(0)

        @pl.when(has_next)
        def _():
            act(1)

        @pl.when(has_previous)
        def _():
            act(-1)

    barrier = pltpu.get_barrier_semaphore()

    def greet(device, level):
        pl.semaphore_signal(barrier, inc=1, device_id=(device, level), device_id_type=MESH)

    @pl.loop(1, planes)
    def _(step):
        greet(phi_of(lax.rem(here + step, planes), half), row)

    greet(phi_of(here, other), lax.rem(row + rows - rows // 2, rows))

    def greet_rows(step):
        if step != 0:
            greet(phi, row + step)
            greet(near, row + step)

    steps(greet_rows)

    @pl.when(half == 0)
    def _():
        steps(lambda step: greet(far, row + step))

    @pl.when(is_root)
    def _():
        @pl.loop(0, column)
        def _(z):
            side, level = lax.div(z, rows), lax.rem(z, rows)
            greet(phi_of(twin, side), level)
            greet(phi_of(place_of(far_of_early), side), level)

            @pl.when(z != 0)
            def _():
                greet(phi_of(here, side), level)

    for index in range(3):
        inputs[index].wait()
    owner = owner_ref[...]
    target = (owner >> 2) * 32 + (owner & 1) * 16 + ((owner >> 1) & 1) * 8 + offset_ref[...]
    slot = lax.broadcasted_iota(jnp.int32, (slots, owner.shape[1]), 0)
    chosen = jnp.where(slot == target, 1.0, 0.0).astype(BF16)
    packed = jnp.dot(chosen, mag_ref[...], preferred_element_type=F32).astype(BF16)
    pack[...] = packed.reshape(planes, 2 * CAP, width)
    recv[here] = pack[here]

    inputs[3].wait()
    weights = weight_ref[...]
    from_slot = lax.broadcasted_iota(jnp.int32, (slots, planes * CAP), 0)
    to_slot = lax.broadcasted_iota(jnp.int32, (slots, planes * CAP), 1)
    source = to_slot >> 3
    natural = ((source >> 1) * 4 + other * 2 + (source & 1)) * CAP + (to_slot & 7)
    pick = jnp.where(from_slot == natural, 1.0, 0.0).astype(BF16)
    wsend[...] = jnp.dot(weights, pick, preferred_element_type=F32).astype(BF16)
    inputs[4].wait()

    def flag(condition):
        return jnp.where(condition, 1, 0).astype(jnp.int32)

    pl.semaphore_wait(
        barrier,
        (planes - 1)
        + 1
        + 2 * (flag(has_next) + flag(has_previous))
        + half * (1 + flag(has_next) + flag(has_previous))
        + 2
        + flag(depth != 0),
    )

    def remote(src, dst, send, receive, device, level):
        return pltpu.make_async_remote_copy(
            src_ref=src,
            dst_ref=dst,
            send_sem=send,
            recv_sem=receive,
            device_id=(device, level),
            device_id_type=MESH,
        )

    weight_copy = remote(
        wsend, wrecv, w_send, w_recv, phi_of(here, other), lax.rem(row + rows // 2, rows)
    )
    weight_copy.start()

    def pack_copy(place, slot):
        return remote(
            pack.at[place],
            recv.at[slot],
            pack_send.at[place],
            pack_recv.at[slot],
            phi_of(place, half),
            row,
        )

    @pl.loop(1, planes)
    def _(step):
        pack_copy(lax.rem(here + step, planes), here).start()

    def layers_of(step):
        if step == 0:
            return pl.ds(EDGE, layers), pl.ds(EDGE, layers)
        if step > 0:
            return pl.ds(layers, EDGE), pl.ds(0, EDGE)
        return pl.ds(EDGE, EDGE), pl.ds(EDGE + layers, EDGE)

    def radial_copy(step):
        source, ghost = layers_of(step)
        return remote(
            mid.at[source],
            mid.at[ghost],
            radial_send.at[1 + step],
            radial_recv.at[1 - step],
            phi,
            row + step,
        )

    def near_copy(step):
        source, ghost = layers_of(step)
        return remote(
            mid.at[source, pl.ds(near_src, PAD)],
            near_ghost.at[ghost],
            nghost_send.at[1 + step],
            nghost_recv.at[1 - step],
            near,
            row + step,
        )

    def far_copy(step):
        source, ghost = layers_of(step)
        return remote(
            mid.at[source, pl.ds(far_src, PAD)],
            far_ghost.at[ghost],
            fghost_send.at[1 + step],
            fghost_recv.at[1 - step],
            far,
            row + step,
        )

    def arrival(buffer, semaphore, step):
        _, ghost = layers_of(-step)
        return remote(
            buffer.at[ghost], buffer.at[ghost], w_send, semaphore.at[1 + step], near, row
        )

    def shadow_copies(step):
        if step == 0:
            source, ghost = pl.ds(EDGE, layers), pl.ds(EDGE, layers)
        else:
            source, ghost = pl.ds(EDGE, EDGE), pl.ds(EDGE + layers, EDGE)
        return (
            remote(
                mid.at[source],
                shadow_mid.at[ghost],
                shadow_send.at[0],
                shadow_recv.at[2 * step],
                early_phi,
                0,
            ),
            remote(
                mid.at[source, pl.ds(near_src, PAD)],
                shadow_near.at[ghost],
                shadow_send.at[1],
                shadow_recv.at[2 * step + 1],
                early_twin_phi,
                0,
            ),
        )

    def shadow_do(act):
        for step in (0, 1):

            @pl.when(depth == rows + step)
            def _():
                for copy in shadow_copies(step):
                    act(copy)

    @pl.when(half == 1)
    def _():
        steps(lambda step: far_copy(step).start())

    shadow_do(lambda copy: copy.start())

    def row_copies(step):
        if step != 0:
            radial_copy(step).start()
        near_copy(step).start()

    steps(row_copies)

    for index in range(5, 9):
        inputs[index].wait()
    lanes = lax.broadcasted_iota(jnp.int32, (tall, width), 1)
    theta_coef = jnp.broadcast_to(theta_coef_ref[...], (tall, width))
    theta_upper = jnp.where(lanes < width - 1, 0.5 * (theta_coef + roll(theta_coef, -1, 1)), 0.0)
    theta_lower = jnp.where(lanes > 0, roll(theta_upper, 1, 1), 0.0)
    lines = phi_coef_ref.shape[0]
    lane8 = lax.broadcasted_iota(jnp.int32, (8, width), 1)
    top_index = layers * rows - 1

    def radial_faces(level):
        def coef_at(index):
            return radial_ref[jnp.clip(index, 0, top_index)]

        return [
            0.5
            * (
                coef_at(level * layers + i - EDGE - 1)
                + coef_at(level * layers + i - EDGE)
            )
            for i in range(deep + 1)
        ]

    def inside(level, i):
        index = level * layers + i - EDGE
        return jnp.logical_and(index >= 0, index <= top_index)

    def set_faces(which, slab, level):
        first = lax.rem(slab * cells - PAD + lines * width, lines * width)
        line = lax.div(first, width)
        shift = width - lax.rem(first, width)
        near_line = phi_coef_ref[pl.ds(line, 1), :]
        next_line = phi_coef_ref[pl.ds(lax.rem(line + 1, lines), 1), :]
        window = jnp.where(
            lane8 < shift,
            pltpu.roll(jnp.broadcast_to(near_line, (8, width)), shift, 1),
            pltpu.roll(jnp.broadcast_to(next_line, (8, width)), shift, 1),
        )
        phi_face = 0.5 * (window + roll(window, -1, 1))
        phi_upper = jnp.broadcast_to(phi_face[0:1], (width, width)).T[:tall]
        phi_lower = roll(phi_upper, 1, 0)
        faces[which, 0] = phi_upper
        faces[which, 1] = phi_lower
        radial = radial_faces(level)
        around = phi_upper + phi_lower + theta_upper + theta_lower
        for i in range(1, deep - 1):
            weight = jnp.where(inside(level, i), 1.0, 0.0).astype(F32)
            inverse[which, i] = weight / (radial[i] + radial[i + 1] + around)

    def image(which, radial, cell, i):
        phi_upper, phi_lower = faces[which, 0], faces[which, 1]
        value = cell(i)
        result = radial[i + 1] * (value - cell(i + 1))
        result = result + radial[i] * (value - cell(i - 1))
        result = result + theta_upper * (value - roll(value, -1, 1))
        result = result + theta_lower * (value - roll(value, 1, 1))
        result = result + phi_upper * (value - roll(value, -1, 0))
        return result + phi_lower * (value - roll(value, 1, 0))

    def at(which, kind):
        return lambda i: values[which, kind, i]

    def evaluate(which, level):
        radial = radial_faces(level)
        for i in range(1, deep - 1):
            residual = -image(which, radial, lambda j: field[which, j], i)
            values[which, 0, i] = residual
            values[which, 1, i] = residual * inverse[which, i]
        for i in range(2, deep - 2):
            first = image(which, radial, at(which, 1), i)
            values[which, 2, i] = first
            values[which, 3, i] = first * inverse[which, i]
        for i in range(3, deep - 3):
            values[which, 4, i] = image(which, radial, at(which, 3), i)

    def add_boundary(which, boundary):
        radial = radial_faces(0)
        residual = values[which, 0, EDGE] + radial[EDGE] * boundary
        values[which, 0, EDGE] = residual
        values[which, 1, EDGE] = residual * inverse[which, EDGE]
        for i in (EDGE, EDGE + 1):
            first = image(which, radial, at(which, 1), i)
            values[which, 2, i] = first
            values[which, 3, i] = first * inverse[which, i]
        for i in (EDGE, EDGE + 1, EDGE + 2):
            values[which, 4, i] = image(which, radial, at(which, 3), i)

    cell_index = lax.broadcasted_iota(jnp.int32, (tall, width), 0)
    lane = lax.broadcasted_iota(jnp.int32, (1, width), 1)

    def inner_sums(which, side):
        reach = EDGE * (1 - 2 * side)
        low = PAD - (1 - core) * reach
        high = PAD + cells + core * reach
        counted = jnp.logical_and(cell_index >= low, cell_index < high)
        result = jnp.zeros((1, width), F32)
        for index, (left, right) in enumerate(((0, 1), (1, 2), (2, 3), (3, 4))):
            total = None
            for i in range(EDGE, EDGE + layers):
                product = values[which, left, i] * values[which, right, i]
                total = product if total is None else total + product
            total = jnp.where(counted, total, 0.0)
            total = jnp.sum(total, axis=0, keepdims=True)
            total = jnp.sum(total, axis=1, keepdims=True)
            result = jnp.where(lane == index, total, result)
        return result

    def assemble(which, middle, near_cells, far_cells, level):
        for i in range(deep):
            keep = inside(level, i)
            near_value = jnp.where(keep, near_cells[i], 0.0)
            far_value = jnp.zeros_like(near_value)
            if far_cells is not None:
                far_value = jnp.where(keep, far_cells[i], 0.0)
            field[which, i, 0:PAD] = jnp.where(core == 0, far_value, near_value)
            field[which, i, PAD + cells : tall] = jnp.where(core == 0, near_value, far_value)
            field[which, i, PAD : PAD + cells] = jnp.where(keep, middle[i], 0.0)

    set_faces(0, phi, row)

    wide = (slots, slots)
    from_slot = lax.broadcasted_iota(jnp.int32, wide, 0)
    to_slot = lax.broadcasted_iota(jnp.int32, wide, 1)
    source = to_slot >> 4
    natural = ((source >> 1) * 4 + half * 2 + (source & 1)) * CAP + (to_slot & 7)
    mine = jnp.logical_and(from_slot == natural, ((to_slot >> 3) & 1) == half)
    own_weights = jnp.dot(
        weights, jnp.where(mine, 1.0, 0.0).astype(BF16), preferred_element_type=F32
    )
    from_slot = lax.broadcasted_iota(jnp.int32, (planes * CAP, slots), 0)
    to_slot = lax.broadcasted_iota(jnp.int32, (planes * CAP, slots), 1)
    theirs = jnp.logical_and(
        from_slot == (to_slot >> 4) * CAP + (to_slot & 7), ((to_slot >> 3) & 1) == other
    )
    theirs = jnp.where(theirs, 1.0, 0.0).astype(BF16)
    theta = theta_ref[...].astype(F32)
    weight_copy.wait_recv()
    partner_weights = jnp.dot(wrecv[...], theirs, preferred_element_type=F32)
    both_weights = jnp.concatenate(
        [
            jnp.where(half == 0, own_weights, partner_weights),
            jnp.where(half == 0, partner_weights, own_weights),
        ],
        axis=0,
    ).astype(BF16)

    @pl.loop(1, planes)
    def _(step):
        place = lax.rem(here + step, planes)
        pack_copy(place, place).wait_recv()

    columns = jnp.dot(
        both_weights, recv[...].reshape(slots, width), preferred_element_type=F32
    )
    product = jnp.dot(
        columns, theta, preferred_element_type=F32, precision=lax.Precision.HIGHEST
    )
    part[...] = product.reshape(2, cells, width)

    main_copy = remote(part, main.at[depth], part_send.at[0], main_recv.at[depth], early_phi, 0)
    near_part_copy = remote(
        part.at[:, pl.ds(near_src, PAD)],
        near_part.at[depth],
        part_send.at[1],
        near_recv.at[depth],
        early_twin_phi,
        0,
    )
    far_part_copy = remote(
        part.at[1, pl.ds(far_src, PAD)],
        far_part.at[depth],
        part_send.at[2],
        far_recv.at[depth],
        far_of_late,
        0,
    )
    far_part_copy.start()
    near_part_copy.start()

    @pl.when(depth != 0)
    def _():
        main_copy.start()

    def wait_rows(step):
        if step != 0:
            arrival(mid, radial_recv, step).wait_recv()
        arrival(near_ghost, nghost_recv, step).wait_recv()

    steps(wait_rows)

    @pl.when(half == 0)
    def _():
        def back(step):
            arrival(far_ghost, fghost_recv, step).wait_recv()
            far_copy(step).start()

        steps(back)
        assemble(0, mid, near_ghost, far_ghost, row)

    @pl.when(half == 1)
    def _():
        assemble(0, mid, near_ghost, None, row)

    evaluate(0, row)

    column_copy = remote(
        sums.at[0], sums_column.at[depth], column_send, column_recv.at[depth], early_phi, 0
    )

    @pl.when(depth != 0)
    def _():
        own = inner_sums(0, half)
        sums[0] = jnp.where(is_second, 0.0, own)
        column_copy.start()

    def total_copy(z):
        return remote(
            totals,
            totals,
            total_send.at[z],
            total_recv,
            phi_of(here, lax.div(z, rows)),
            lax.rem(z, rows),
        )

    def plane_copy(place, slot):
        return remote(
            sums.at[1],
            sums_plane.at[slot],
            plane_send.at[place],
            plane_recv.at[slot],
            phi_of(place, 0),
            0,
        )

    forward_copy = remote(
        bound.at[1], forward, forward_send.at[0], forward_recv.at[0], late_phi, 0
    )
    far_forward_copy = remote(
        bound.at[0, pl.ds(pl.multiple_of(PAD + far_src, PAD), PAD)],
        far_forward,
        forward_send.at[1],
        forward_recv.at[1],
        far_of_early,
        0,
    )

    def send_fields():
        copy = pltpu.make_async_copy(
            values.at[0, :, EDGE : EDGE + layers, PAD : PAD + cells], fields_out, out_sem.at[0]
        )
        return copy

    def sides(near_value, far_value):
        return (
            jnp.where(core == 0, far_value, near_value),
            jnp.where(core == 0, near_value, far_value),
        )

    @pl.when(is_root)
    def _():
        set_faces(1, late_phi, 0)
        for step in (0, 1):
            for copy in shadow_copies(step):
                copy.wait_recv()
        assemble(1, shadow_mid, shadow_near, None, 0)
        evaluate(1, 0)
        main[0] = part[...]

        @pl.loop(1, column)
        def _(z):
            remote(
                sums.at[0], sums_column.at[z], column_send, column_recv.at[z], phi, 0
            ).wait_recv()

        @pl.loop(0, column)
        def _(z):
            remote(
                near_part.at[z], near_part.at[z], part_send.at[1], near_recv.at[z], phi, 0
            ).wait_recv()
            remote(
                far_part.at[z], far_part.at[z], part_send.at[2], far_recv.at[z], phi, 0
            ).wait_recv()

            @pl.when(z != 0)
            def _():
                remote(part, main.at[z], part_send.at[0], main_recv.at[z], phi, 0).wait_recv()

        middle = jnp.sum(main[...], axis=0)
        nears = jnp.sum(near_part[...], axis=0)
        fars = jnp.sum(far_part[...], axis=0)
        for which in (0, 1):
            low, high = sides(nears[which], fars if which == 0 else jnp.zeros_like(fars))
            bound[which, 0:PAD] = low
            bound[which, PAD : PAD + cells] = middle[which]
            bound[which, PAD + cells : tall] = high
            add_boundary(which, bound[which])
        sums_column[0] = inner_sums(0, 0) + inner_sums(1, 1)
        mine = jnp.sum(sums_column[...], axis=0)
        sums[1] = mine
        sums_plane[here] = mine

        @pl.loop(1, planes)
        def _(step):
            plane_copy(lax.rem(here + step, planes), here).start()

        forward_copy.start()
        far_forward_copy.start()
        send_fields().start()

        @pl.loop(1, planes)
        def _(step):
            place = lax.rem(here + step, planes)
            plane_copy(place, place).wait_recv()

        totals[...] = jnp.sum(sums_plane[...], axis=0)

        @pl.loop(1, column)
        def _(z):
            total_copy(z).start()

    @pl.when(half == 1)
    def _():
        steps(lambda step: arrival(far_ghost, fghost_recv, step).wait_recv())
        assemble(0, mid, near_ghost, far_ghost, row)
        evaluate(0, row)

    @pl.when(is_second)
    def _():
        forward_copy.wait_recv()
        far_forward_copy.wait_recv()
        boundary = forward[...]
        edge = jnp.where(core == 0, far_forward[...], boundary[0:PAD])
        other_edge = jnp.where(core == 0, boundary[PAD + cells :], far_forward[...])
        add_boundary(
            0, jnp.concatenate([edge, boundary[PAD : PAD + cells], other_edge], axis=0)
        )

    @pl.when(depth != 0)
    def _():
        send_fields().start()
        remote(totals, totals, total_send.at[0], total_recv, phi, 0).wait_recv()

    total = totals[...]
    rz, pq, qw, wt = (
        jnp.sum(jnp.where(lane == index, total, 0.0), axis=1, keepdims=True)
        for index in range(4)
    )
    step0 = rz / pq
    rz_next = step0 * step0 * qw - rz
    ratio = 1.0 + rz_next / rz
    step1 = rz_next / (step0 * step0 * wt - ratio * ratio * pq)
    along = step0 + step1 * ratio
    across = step0 * step1
    coef_out[0:1] = jnp.broadcast_to(along, (1, width))
    coef_out[1:2] = jnp.broadcast_to(across, (1, width))

    send_fields().wait()
    weight_copy.wait_send()

    @pl.loop(1, planes)
    def _(step):
        pack_copy(lax.rem(here + step, planes), here).wait_send()

    def sent_rows(step):
        if step != 0:
            radial_copy(step).wait_send()
        near_copy(step).wait_send()
        far_copy(step).wait_send()

    steps(sent_rows)
    shadow_do(lambda copy: copy.wait_send())
    near_part_copy.wait_send()
    far_part_copy.wait_send()

    @pl.when(depth != 0)
    def _():
        main_copy.wait_send()
        column_copy.wait_send()

    @pl.when(is_root)
    def _():
        forward_copy.wait_send()
        far_forward_copy.wait_send()

        @pl.loop(1, planes)
        def _(step):
            plane_copy(lax.rem(here + step, planes), here).wait_send()

        @pl.loop(1, column)
        def _(z):
            total_copy(z).wait_send()


def body(
    magnetogram,
    col_owner,
    col_offset,
    phi_weight,
    theta_weight,
    radial_coef,
    theta_coef,
    phi_coef,
    start_field,
):
    phis, rows = lax.axis_size("phi"), lax.axis_size("row")
    layers, cells, width = start_field.shape
    planes, column = phis // 2, 2 * rows
    slots = phis * CAP
    tall = cells + 2 * PAD
    deep = layers + 2 * EDGE
    dma = pltpu.SemaphoreType.DMA
    anywhere = pl.BlockSpec(memory_space=pl.ANY)
    operands = (
        magnetogram,
        col_owner.reshape(1, -1),
        col_offset.reshape(1, -1),
        phi_weight.T,
        theta_weight,
        radial_coef,
        theta_coef.reshape(1, -1),
        phi_coef.reshape(-1, width),
        start_field,
    )
    local = [pltpu.VMEM(x.shape, x.dtype) for x in operands[:8]]
    local[5] = pltpu.SMEM(radial_coef.shape, F32)
    fields, coef = pl.pallas_call(
        functools.partial(kernel, phis, rows),
        out_shape=(
            jax.ShapeDtypeStruct((5,) + start_field.shape, F32),
            jax.ShapeDtypeStruct((2, width), F32),
        ),
        in_specs=[anywhere] * 9,
        out_specs=(anywhere, pl.BlockSpec(memory_space=pltpu.VMEM)),
        scratch_shapes=local
        + [
            pltpu.VMEM((planes, 2 * CAP, width), BF16),
            pltpu.VMEM((planes, 2 * CAP, width), BF16),
            pltpu.VMEM((cells, planes * CAP), BF16),
            pltpu.VMEM((cells, planes * CAP), BF16),
            pltpu.VMEM((2, cells, width), F32),
            pltpu.VMEM((column, 2, cells, width), F32),
            pltpu.VMEM((column, 2, PAD, width), F32),
            pltpu.VMEM((column, PAD, width), F32),
            pltpu.VMEM((2, tall, width), F32),
            pltpu.VMEM((tall, width), F32),
            pltpu.VMEM((PAD, width), F32),
            pltpu.VMEM((deep, cells, width), F32),
            pltpu.VMEM((deep, PAD, width), F32),
            pltpu.VMEM((deep, PAD, width), F32),
            pltpu.VMEM((deep, cells, width), F32),
            pltpu.VMEM((deep, PAD, width), F32),
            pltpu.VMEM((2, deep, tall, width), F32),
            pltpu.VMEM((2, deep, tall, width), F32),
            pltpu.VMEM((2, 2, tall, width), F32),
            pltpu.VMEM((2, 5, deep, tall, width), F32),
            pltpu.VMEM((2, 1, width), F32),
            pltpu.VMEM((column, 1, width), F32),
            pltpu.VMEM((planes, 1, width), F32),
            pltpu.VMEM((1, width), F32),
            dma((9,)),
            dma((1,)),
            dma((planes,)),
            dma((planes,)),
            dma,
            dma,
            dma((3,)),
            dma((column,)),
            dma((column,)),
            dma((column,)),
            dma((2,)),
            dma((2,)),
            dma((3,)),
            dma((3,)),
            dma((3,)),
            dma((3,)),
            dma((3,)),
            dma((3,)),
            dma((2,)),
            dma((4,)),
            dma,
            dma((column,)),
            dma((planes,)),
            dma((planes,)),
            dma((column,)),
            dma,
        ],
        compiler_params=pltpu.CompilerParams(collective_id=0, has_side_effects=True),
    )(*operands)
    along, across = coef[0], coef[1]
    solution_field = start_field + along * fields[1] - across * fields[3]
    residual = fields[0] - along * fields[2] + across * fields[4]
    return solution_field, residual


def solution(mesh):
    in_specs = (
        P("phi", "row"),
        P("phi"),
        P("phi"),
        P(None, "phi"),
        P("row", None),
        P(),
        P(),
        P(),
        P("row", "phi", None),
    )
    out_specs = (P("row", "phi", None), P("row", "phi", None))
    return jax.shard_map(body, mesh=mesh, in_specs=in_specs, out_specs=out_specs, check_vma=False)
```

```python
import functools

import jax
import jax.numpy as jnp
from jax import lax
from jax.experimental import pallas as pl
from jax.experimental.pallas import tpu as pltpu
from jax.sharding import PartitionSpec as P

MESH = pl.DeviceIdType.MESH
CAP = 8
PAD = 8
EDGE = 3
F32 = jnp.float32
BF16 = jnp.bfloat16


def roll(x, shift, axis):
    return pltpu.roll(x, shift % x.shape[axis], axis)


def kernel(
    phis,
    rows,
    mag_hbm,
    owner_hbm,
    offset_hbm,
    weight_hbm,
    theta_hbm,
    radial_hbm,
    theta_coef_hbm,
    phi_coef_hbm,
    start_hbm,
    fields_out,
    coef_out,
    mag_ref,
    owner_ref,
    offset_ref,
    weight_ref,
    theta_ref,
    radial_ref,
    theta_coef_ref,
    phi_coef_ref,
    pack,
    recv,
    wsend,
    wrecv,
    part,
    main,
    near_part,
    far_part,
    bound,
    forward,
    far_forward,
    mid,
    near_ghost,
    far_ghost,
    shadow_mid,
    shadow_near,
    field,
    inverse,
    faces,
    values,
    sums,
    sums_column,
    sums_plane,
    totals,
    in_sem,
    pack_send,
    pack_recv,
    w_send,
    w_recv,
    part_send,
    main_recv,
    near_recv,
    far_recv,
    forward_send,
    forward_recv,
    radial_send,
    radial_recv,
    nghost_send,
    nghost_recv,
    fghost_send,
    fghost_recv,
    shadow_send,
    shadow_recv,
    column_send,
    column_recv,
    plane_send,
    plane_recv,
    total_send,
    total_recv,
):
    phi = lax.axis_index("phi")
    row = lax.axis_index("row")
    planes = phis // 2
    column = 2 * rows
    layers = start_hbm.shape[0]
    cells = start_hbm.shape[1]
    width = start_hbm.shape[2]
    tall = cells + 2 * PAD
    deep = layers + 2 * EDGE
    core = lax.rem(phi, 2)
    half = lax.rem(lax.div(phi, 2), 2)
    other = 1 - half
    here = lax.div(phi, 4) * 2 + core
    depth = half * rows + row
    slots = planes * 2 * CAP
    is_root = depth == 0
    is_second = depth == rows

    offsets = (1, 2, 4)
    reach = jnp.where(half == 0, row, column - depth)
    bit = jnp.where(
        lax.rem(reach, 2) == 1, 1, jnp.where(lax.rem(reach, 4) == 2, 2, 4)
    ).astype(jnp.int32)
    bit = jnp.where(reach == rows, 2, bit).astype(jnp.int32)
    parent_reach = jnp.where(reach == rows, rows - 2, reach - bit).astype(jnp.int32)
    is_feeder = jnp.logical_and(parent_reach == 0, depth != 0)
    parent_half = jnp.where(parent_reach == 0, 0, half).astype(jnp.int32)
    parent_depth = jnp.where(half == 0, parent_reach, column - parent_reach)
    parent_depth = jnp.where(parent_reach == 0, 0, parent_depth).astype(jnp.int32)
    parent_row = parent_depth - parent_half * rows
    tree_slot = lax.div(bit, 2) + jnp.where(is_feeder, 3 * half, 0).astype(jnp.int32)
    inner = jnp.logical_and(reach > 0, reach < rows)
    has_child = (
        jnp.logical_and(inner, jnp.logical_and(lax.rem(reach, 2) == 0, reach + 1 < rows)),
        jnp.logical_and(
            inner,
            jnp.logical_or(
                jnp.logical_and(lax.rem(reach, 4) == 0, reach + 2 < rows),
                jnp.logical_and(half == 1, reach == rows - 2),
            ),
        ),
    )
    child_depth = [
        jnp.where(half == 0, depth + offset, depth - offset).astype(jnp.int32)
        for offset in offsets[:2]
    ]
    feeders = [(0, 0)]
    for index, offset in enumerate(offsets):
        if offset < rows:
            feeders += [(offset, 1 + index), (column - offset, 4 + index)]
        elif offset == rows == 2:
            feeders.append((column - offset, 4 + index))
    feeder_slot = jnp.where(is_feeder, 1 + tree_slot, 0).astype(jnp.int32)

    def phi_of(place, side):
        return lax.div(place, 2) * 4 + side * 2 + lax.rem(place, 2)

    def wrap(index):
        return lax.rem(index + phis, phis)

    def place_of(index):
        return lax.div(index, 4) * 2 + lax.rem(index, 2)

    twin = here + 1 - 2 * core
    near = phi + 1 - 2 * core
    far_step = 2 * core - 1
    far = wrap(phi + far_step)
    early_phi, late_phi = phi_of(here, 0), phi_of(here, 1)
    far_of_early, far_of_late = wrap(early_phi + far_step), wrap(late_phi + far_step)
    early_twin_phi = phi_of(twin, 0)
    last = cells - PAD
    near_src = pl.multiple_of((1 - core) * last, PAD)
    far_src = pl.multiple_of(core * last, PAD)

    inputs = [
        pltpu.make_async_copy(src, dst, in_sem.at[index])
        for index, (src, dst) in enumerate(
            (
                (owner_hbm, owner_ref),
                (offset_hbm, offset_ref),
                (mag_hbm, mag_ref),
                (weight_hbm, weight_ref),
                (start_hbm, mid.at[EDGE : EDGE + layers]),
                (radial_hbm, radial_ref),
                (theta_coef_hbm, theta_coef_ref),
                (phi_coef_hbm, phi_coef_ref),
                (theta_hbm, theta_ref),
            )
        )
    ]
    for copy in inputs:
        copy.start()

    has_next = row < rows - 1
    has_previous = row > 0

    def steps(act):
        act(0)

        @pl.when(has_next)
        def _():
            act(1)

        @pl.when(has_previous)
        def _():
            act(-1)

    barrier = pltpu.get_barrier_semaphore()

    def greet(device, level):
        pl.semaphore_signal(barrier, inc=1, device_id=(device, level), device_id_type=MESH)

    @pl.loop(1, planes)
    def _(step):
        greet(phi_of(lax.rem(here + step, planes), half), row)

    greet(phi_of(here, other), lax.rem(row + rows - rows // 2, rows))

    def greet_rows(step):
        if step != 0:
            greet(phi, row + step)
            greet(near, row + step)

    steps(greet_rows)

    @pl.when(half == 0)
    def _():
        steps(lambda step: greet(far, row + step))

    @pl.when(is_root)
    def _():
        for z, _slot in feeders:
            side, level = z // rows, z % rows
            greet(phi_of(twin, side), level)
            greet(phi_of(place_of(far_of_early), side), level)

        for step in (0, 1):
            greet(phi_of(twin, 1), step)

        @pl.loop(1, column)
        def _(z):
            greet(phi_of(here, lax.div(z, rows)), lax.rem(z, rows))

    for index in range(2):

        @pl.when(has_child[index])
        def _():
            greet(phi, child_depth[index] - half * rows)

    for index in range(3):
        inputs[index].wait()
    owner = owner_ref[...]
    target = (owner >> 2) * 32 + (owner & 1) * 16 + ((owner >> 1) & 1) * 8 + offset_ref[...]
    slot = lax.broadcasted_iota(jnp.int32, (slots, owner.shape[1]), 0)
    chosen = jnp.where(slot == target, 1.0, 0.0).astype(BF16)
    packed = jnp.dot(chosen, mag_ref[...], preferred_element_type=F32).astype(BF16)
    pack[...] = packed.reshape(planes, 2 * CAP, width)
    recv[here] = pack[here]

    inputs[3].wait()
    weights = weight_ref[...]
    from_slot = lax.broadcasted_iota(jnp.int32, (slots, planes * CAP), 0)
    to_slot = lax.broadcasted_iota(jnp.int32, (slots, planes * CAP), 1)
    source = to_slot >> 3
    natural = ((source >> 1) * 4 + other * 2 + (source & 1)) * CAP + (to_slot & 7)
    pick = jnp.where(from_slot == natural, 1.0, 0.0).astype(BF16)
    wsend[...] = jnp.dot(weights, pick, preferred_element_type=F32).astype(BF16)
    inputs[4].wait()

    def flag(condition):
        return jnp.where(condition, 1, 0).astype(jnp.int32)

    pl.semaphore_wait(
        barrier,
        (planes - 1)
        + 1
        + 2 * (flag(has_next) + flag(has_previous))
        + half * (1 + flag(has_next) + flag(has_previous))
        + flag(depth != 0)
        + 2 * flag(jnp.logical_or(is_feeder, is_root))
        + flag(jnp.logical_and(depth != 0, parent_reach != 0))
        + flag(jnp.logical_or(depth == rows, depth == rows + 1)),
    )

    def remote(src, dst, send, receive, device, level):
        return pltpu.make_async_remote_copy(
            src_ref=src,
            dst_ref=dst,
            send_sem=send,
            recv_sem=receive,
            device_id=(device, level),
            device_id_type=MESH,
        )

    weight_copy = remote(
        wsend, wrecv, w_send, w_recv, phi_of(here, other), lax.rem(row + rows // 2, rows)
    )
    weight_copy.start()

    def pack_copy(place, slot):
        return remote(
            pack.at[place],
            recv.at[slot],
            pack_send.at[place],
            pack_recv.at[slot],
            phi_of(place, half),
            row,
        )

    @pl.loop(1, planes)
    def _(step):
        pack_copy(lax.rem(here + step, planes), here).start()

    def layers_of(step):
        if step == 0:
            return pl.ds(EDGE, layers), pl.ds(EDGE, layers)
        if step > 0:
            return pl.ds(layers, EDGE), pl.ds(0, EDGE)
        return pl.ds(EDGE, EDGE), pl.ds(EDGE + layers, EDGE)

    def radial_copy(step):
        source, ghost = layers_of(step)
        return remote(
            mid.at[source],
            mid.at[ghost],
            radial_send.at[1 + step],
            radial_recv.at[1 - step],
            phi,
            row + step,
        )

    def near_copy(step):
        source, ghost = layers_of(step)
        return remote(
            mid.at[source, pl.ds(near_src, PAD)],
            near_ghost.at[ghost],
            nghost_send.at[1 + step],
            nghost_recv.at[1 - step],
            near,
            row + step,
        )

    def far_copy(step):
        source, ghost = layers_of(step)
        return remote(
            mid.at[source, pl.ds(far_src, PAD)],
            far_ghost.at[ghost],
            fghost_send.at[1 + step],
            fghost_recv.at[1 - step],
            far,
            row + step,
        )

    def arrival(buffer, semaphore, step):
        _, ghost = layers_of(-step)
        return remote(
            buffer.at[ghost], buffer.at[ghost], w_send, semaphore.at[1 + step], near, row
        )

    def shadow_copies(step):
        if step == 0:
            source, ghost = pl.ds(EDGE, layers), pl.ds(EDGE, layers)
        else:
            source, ghost = pl.ds(EDGE, EDGE), pl.ds(EDGE + layers, EDGE)
        return (
            remote(
                mid.at[source],
                shadow_mid.at[ghost],
                shadow_send.at[0],
                shadow_recv.at[2 * step],
                early_phi,
                0,
            ),
            remote(
                mid.at[source, pl.ds(near_src, PAD)],
                shadow_near.at[ghost],
                shadow_send.at[1],
                shadow_recv.at[2 * step + 1],
                early_twin_phi,
                0,
            ),
        )

    def shadow_do(act):
        for step in (0, 1):

            @pl.when(depth == rows + step)
            def _():
                for copy in shadow_copies(step):
                    act(copy)

    @pl.when(half == 1)
    def _():
        steps(lambda step: far_copy(step).start())

    def row_copies(step):
        if step != 0:
            radial_copy(step).start()
        near_copy(step).start()

    steps(row_copies)
    shadow_do(lambda copy: copy.start())

    for index in range(5, 9):
        inputs[index].wait()
    lanes = lax.broadcasted_iota(jnp.int32, (tall, width), 1)
    theta_coef = jnp.broadcast_to(theta_coef_ref[...], (tall, width))
    theta_upper = jnp.where(lanes < width - 1, 0.5 * (theta_coef + roll(theta_coef, -1, 1)), 0.0)
    theta_lower = jnp.where(lanes > 0, roll(theta_upper, 1, 1), 0.0)
    lines = phi_coef_ref.shape[0]
    lane8 = lax.broadcasted_iota(jnp.int32, (8, width), 1)
    top_index = layers * rows - 1

    def radial_faces(level):
        def coef_at(index):
            return radial_ref[jnp.clip(index, 0, top_index)]

        return [
            0.5
            * (
                coef_at(level * layers + i - EDGE - 1)
                + coef_at(level * layers + i - EDGE)
            )
            for i in range(deep + 1)
        ]

    def inside(level, i):
        index = level * layers + i - EDGE
        return jnp.logical_and(index >= 0, index <= top_index)

    def set_faces(which, slab, level):
        first = lax.rem(slab * cells - PAD + lines * width, lines * width)
        line = lax.div(first, width)
        shift = width - lax.rem(first, width)
        near_line = phi_coef_ref[pl.ds(line, 1), :]
        next_line = phi_coef_ref[pl.ds(lax.rem(line + 1, lines), 1), :]
        window = jnp.where(
            lane8 < shift,
            pltpu.roll(jnp.broadcast_to(near_line, (8, width)), shift, 1),
            pltpu.roll(jnp.broadcast_to(next_line, (8, width)), shift, 1),
        )
        phi_face = 0.5 * (window + roll(window, -1, 1))
        phi_upper = jnp.broadcast_to(phi_face[0:1], (width, width)).T[:tall]
        phi_lower = roll(phi_upper, 1, 0)
        faces[which, 0] = phi_upper
        faces[which, 1] = phi_lower
        radial = radial_faces(level)
        around = phi_upper + phi_lower + theta_upper + theta_lower
        for i in range(1, deep - 1):
            weight = jnp.where(inside(level, i), 1.0, 0.0).astype(F32)
            inverse[which, i] = weight / (radial[i] + radial[i + 1] + around)

    def image(which, radial, cell, i):
        phi_upper, phi_lower = faces[which, 0], faces[which, 1]
        value = cell(i)
        result = radial[i + 1] * (value - cell(i + 1))
        result = result + radial[i] * (value - cell(i - 1))
        result = result + theta_upper * (value - roll(value, -1, 1))
        result = result + theta_lower * (value - roll(value, 1, 1))
        result = result + phi_upper * (value - roll(value, -1, 0))
        return result + phi_lower * (value - roll(value, 1, 0))

    def at(which, kind):
        return lambda i: values[which, kind, i]

    def evaluate(which, level):
        radial = radial_faces(level)
        for i in range(1, deep - 1):
            residual = -image(which, radial, lambda j: field[which, j], i)
            values[which, 0, i] = residual
            values[which, 1, i] = residual * inverse[which, i]
        for i in range(2, deep - 2):
            first = image(which, radial, at(which, 1), i)
            values[which, 2, i] = first
            values[which, 3, i] = first * inverse[which, i]
        for i in range(3, deep - 3):
            values[which, 4, i] = image(which, radial, at(which, 3), i)

    def add_boundary(which, boundary):
        radial = radial_faces(0)
        residual = values[which, 0, EDGE] + radial[EDGE] * boundary
        values[which, 0, EDGE] = residual
        values[which, 1, EDGE] = residual * inverse[which, EDGE]
        for i in (EDGE, EDGE + 1):
            first = image(which, radial, at(which, 1), i)
            values[which, 2, i] = first
            values[which, 3, i] = first * inverse[which, i]
        for i in (EDGE, EDGE + 1, EDGE + 2):
            values[which, 4, i] = image(which, radial, at(which, 3), i)

    cell_index = lax.broadcasted_iota(jnp.int32, (tall, width), 0)
    lane = lax.broadcasted_iota(jnp.int32, (1, width), 1)

    def inner_sums(which, side):
        reach = EDGE * (1 - 2 * side)
        low = PAD - (1 - core) * reach
        high = PAD + cells + core * reach
        counted = jnp.logical_and(cell_index >= low, cell_index < high)
        result = jnp.zeros((1, width), F32)
        for index, (left, right) in enumerate(((0, 1), (1, 2), (2, 3), (3, 4))):
            total = None
            for i in range(EDGE, EDGE + layers):
                product = values[which, left, i] * values[which, right, i]
                total = product if total is None else total + product
            total = jnp.where(counted, total, 0.0)
            total = jnp.sum(total, axis=0, keepdims=True)
            total = jnp.sum(total, axis=1, keepdims=True)
            result = jnp.where(lane == index, total, result)
        return result

    def assemble(which, middle, near_cells, far_cells, level):
        for i in range(deep):
            keep = inside(level, i)
            near_value = jnp.where(keep, near_cells[i], 0.0)
            far_value = jnp.zeros_like(near_value)
            if far_cells is not None:
                far_value = jnp.where(keep, far_cells[i], 0.0)
            field[which, i, 0:PAD] = jnp.where(core == 0, far_value, near_value)
            field[which, i, PAD + cells : tall] = jnp.where(core == 0, near_value, far_value)
            field[which, i, PAD : PAD + cells] = jnp.where(keep, middle[i], 0.0)

    set_faces(0, phi, row)
    column_copy = remote(
        sums.at[0], sums_column.at[depth], column_send, column_recv.at[depth], early_phi, 0
    )

    def wait_rows(step):
        if step != 0:
            arrival(mid, radial_recv, step).wait_recv()
        arrival(near_ghost, nghost_recv, step).wait_recv()

    @pl.when(half == 1)
    def _():
        steps(wait_rows)
        assemble(0, mid, near_ghost, None, row)
        evaluate(0, row)
        sums[0] = jnp.where(is_second, 0.0, inner_sums(0, 1))
        column_copy.start()

    wide = (slots, slots)
    from_slot = lax.broadcasted_iota(jnp.int32, wide, 0)
    to_slot = lax.broadcasted_iota(jnp.int32, wide, 1)
    source = to_slot >> 4
    natural = ((source >> 1) * 4 + half * 2 + (source & 1)) * CAP + (to_slot & 7)
    mine = jnp.logical_and(from_slot == natural, ((to_slot >> 3) & 1) == half)
    own_weights = jnp.dot(
        weights, jnp.where(mine, 1.0, 0.0).astype(BF16), preferred_element_type=F32
    )
    from_slot = lax.broadcasted_iota(jnp.int32, (planes * CAP, slots), 0)
    to_slot = lax.broadcasted_iota(jnp.int32, (planes * CAP, slots), 1)
    theirs = jnp.logical_and(
        from_slot == (to_slot >> 4) * CAP + (to_slot & 7), ((to_slot >> 3) & 1) == other
    )
    theirs = jnp.where(theirs, 1.0, 0.0).astype(BF16)
    theta = theta_ref[...].astype(F32)
    weight_copy.wait_recv()
    partner_weights = jnp.dot(wrecv[...], theirs, preferred_element_type=F32)
    both_weights = jnp.concatenate(
        [
            jnp.where(half == 0, own_weights, partner_weights),
            jnp.where(half == 0, partner_weights, own_weights),
        ],
        axis=0,
    ).astype(BF16)

    @pl.loop(1, planes)
    def _(step):
        place = lax.rem(here + step, planes)
        pack_copy(place, place).wait_recv()

    columns = jnp.dot(
        both_weights, recv[...].reshape(slots, width), preferred_element_type=F32
    )
    product = jnp.dot(
        columns, theta, preferred_element_type=F32, precision=lax.Precision.HIGHEST
    )
    part[...] = product.reshape(2, cells, width)

    def child_copy(slot):
        return remote(part, main.at[slot], part_send.at[0], main_recv.at[slot], phi, row)

    for index in range(2):

        @pl.when(has_child[index])
        def _():
            child_copy(index).wait_recv()
            part[...] += main[index]

    main_copy = remote(
        part,
        main.at[tree_slot],
        part_send.at[0],
        main_recv.at[tree_slot],
        phi_of(here, parent_half),
        parent_row,
    )
    near_part_copy = remote(
        part.at[:, pl.ds(near_src, PAD)],
        near_part.at[feeder_slot],
        part_send.at[1],
        near_recv.at[feeder_slot],
        early_twin_phi,
        0,
    )
    far_part_copy = remote(
        part.at[1, pl.ds(far_src, PAD)],
        far_part.at[feeder_slot],
        part_send.at[2],
        far_recv.at[feeder_slot],
        far_of_late,
        0,
    )

    @pl.when(depth != 0)
    def _():
        main_copy.start()

    @pl.when(jnp.logical_or(is_feeder, is_root))
    def _():
        far_part_copy.start()
        near_part_copy.start()

    @pl.when(half == 0)
    def _():
        steps(wait_rows)
        steps(lambda step: arrival(far_ghost, fghost_recv, step).wait_recv())
        assemble(0, mid, near_ghost, far_ghost, row)
        evaluate(0, row)

        @pl.when(depth != 0)
        def _():
            sums[0] = inner_sums(0, 0)
            column_copy.start()

        steps(lambda step: far_copy(step).start())

    def total_copy(z):
        return remote(
            totals,
            totals,
            total_send.at[z],
            total_recv,
            phi_of(here, lax.div(z, rows)),
            lax.rem(z, rows),
        )

    def plane_copy(place, slot):
        return remote(
            sums.at[1],
            sums_plane.at[slot],
            plane_send.at[place],
            plane_recv.at[slot],
            phi_of(place, 0),
            0,
        )

    forward_copy = remote(
        bound.at[1], forward, forward_send.at[0], forward_recv.at[0], late_phi, 0
    )
    far_forward_copy = remote(
        bound.at[0, pl.ds(pl.multiple_of(PAD + far_src, PAD), PAD)],
        far_forward,
        forward_send.at[1],
        forward_recv.at[1],
        far_of_early,
        0,
    )

    def keep_fields():
        for kind in range(5):
            for layer in range(layers):
                fields_out[kind, layer] = values[0, kind, EDGE + layer, PAD : PAD + cells]

    def sides(near_value, far_value):
        return (
            jnp.where(core == 0, far_value, near_value),
            jnp.where(core == 0, near_value, far_value),
        )

    @pl.when(is_root)
    def _():
        set_faces(1, late_phi, 0)
        for step in (0, 1):
            for copy in shadow_copies(step):
                copy.wait_recv()
        assemble(1, shadow_mid, shadow_near, None, 0)
        evaluate(1, 0)

        @pl.loop(1, column)
        def _(z):
            remote(
                sums.at[0], sums_column.at[z], column_send, column_recv.at[z], phi, 0
            ).wait_recv()

        middle, nears, fars = part[...], None, None
        for _z, slot in feeders:
            remote(
                near_part.at[slot], near_part.at[slot], part_send.at[1], near_recv.at[slot], phi, 0
            ).wait_recv()
            remote(
                far_part.at[slot], far_part.at[slot], part_send.at[2], far_recv.at[slot], phi, 0
            ).wait_recv()
            nears = near_part[slot] if nears is None else nears + near_part[slot]
            fars = far_part[slot] if fars is None else fars + far_part[slot]
            if slot:
                child_copy(slot - 1).wait_recv()
                middle = middle + main[slot - 1]
        for which in (0, 1):
            low, high = sides(nears[which], fars if which == 0 else jnp.zeros_like(fars))
            bound[which, 0:PAD] = low
            bound[which, PAD : PAD + cells] = middle[which]
            bound[which, PAD + cells : tall] = high
            add_boundary(which, bound[which])
        sums_column[0] = inner_sums(0, 0) + inner_sums(1, 1)
        mine = jnp.sum(sums_column[...], axis=0)
        sums[1] = mine
        sums_plane[here] = mine

        @pl.loop(1, planes)
        def _(step):
            plane_copy(lax.rem(here + step, planes), here).start()

        forward_copy.start()
        far_forward_copy.start()
        keep_fields()

        @pl.loop(1, planes)
        def _(step):
            place = lax.rem(here + step, planes)
            plane_copy(place, place).wait_recv()

        totals[...] = jnp.sum(sums_plane[...], axis=0)

        @pl.loop(1, column)
        def _(z):
            total_copy(z).start()

    @pl.when(half == 1)
    def _():
        steps(lambda step: arrival(far_ghost, fghost_recv, step).wait_recv())
        assemble(0, mid, near_ghost, far_ghost, row)
        evaluate(0, row)

    @pl.when(is_second)
    def _():
        forward_copy.wait_recv()
        far_forward_copy.wait_recv()
        boundary = forward[...]
        edge = jnp.where(core == 0, far_forward[...], boundary[0:PAD])
        other_edge = jnp.where(core == 0, boundary[PAD + cells :], far_forward[...])
        add_boundary(
            0, jnp.concatenate([edge, boundary[PAD : PAD + cells], other_edge], axis=0)
        )

    @pl.when(depth != 0)
    def _():
        keep_fields()
        remote(totals, totals, total_send.at[0], total_recv, phi, 0).wait_recv()

    total = totals[...]
    rz, pq, qw, wt = (
        jnp.sum(jnp.where(lane == index, total, 0.0), axis=1, keepdims=True)
        for index in range(4)
    )
    step0 = rz / pq
    rz_next = step0 * step0 * qw - rz
    ratio = 1.0 + rz_next / rz
    step1 = rz_next / (step0 * step0 * wt - ratio * ratio * pq)
    along = step0 + step1 * ratio
    across = step0 * step1
    coef_out[0:1] = jnp.broadcast_to(along, (1, width))
    coef_out[1:2] = jnp.broadcast_to(across, (1, width))

    weight_copy.wait_send()

    @pl.loop(1, planes)
    def _(step):
        pack_copy(lax.rem(here + step, planes), here).wait_send()

    def sent_rows(step):
        if step != 0:
            radial_copy(step).wait_send()
        near_copy(step).wait_send()
        far_copy(step).wait_send()

    steps(sent_rows)
    shadow_do(lambda copy: copy.wait_send())

    @pl.when(jnp.logical_or(is_feeder, is_root))
    def _():
        near_part_copy.wait_send()
        far_part_copy.wait_send()

    @pl.when(depth != 0)
    def _():
        main_copy.wait_send()
        column_copy.wait_send()

    @pl.when(is_root)
    def _():
        forward_copy.wait_send()
        far_forward_copy.wait_send()

        @pl.loop(1, planes)
        def _(step):
            plane_copy(lax.rem(here + step, planes), here).wait_send()

        @pl.loop(1, column)
        def _(z):
            total_copy(z).wait_send()


def body(
    magnetogram,
    col_owner,
    col_offset,
    phi_weight,
    theta_weight,
    radial_coef,
    theta_coef,
    phi_coef,
    start_field,
):
    phis, rows = lax.axis_size("phi"), lax.axis_size("row")
    layers, cells, width = start_field.shape
    planes, column = phis // 2, 2 * rows
    slots = phis * CAP
    tall = cells + 2 * PAD
    deep = layers + 2 * EDGE
    dma = pltpu.SemaphoreType.DMA
    anywhere = pl.BlockSpec(memory_space=pl.ANY)
    operands = (
        magnetogram,
        col_owner.reshape(1, -1),
        col_offset.reshape(1, -1),
        phi_weight.T,
        theta_weight,
        radial_coef,
        theta_coef.reshape(1, -1),
        phi_coef.reshape(-1, width),
        start_field,
    )
    local = [pltpu.VMEM(x.shape, x.dtype) for x in operands[:8]]
    local[5] = pltpu.SMEM(radial_coef.shape, F32)
    fields, coef = pl.pallas_call(
        functools.partial(kernel, phis, rows),
        out_shape=(
            pltpu.VMEM((5,) + start_field.shape, F32),
            pltpu.VMEM((2, width), F32),
        ),
        in_specs=[anywhere] * 9,
        out_specs=(pl.BlockSpec(memory_space=pltpu.VMEM),) * 2,
        scratch_shapes=local
        + [
            pltpu.VMEM((planes, 2 * CAP, width), BF16),
            pltpu.VMEM((planes, 2 * CAP, width), BF16),
            pltpu.VMEM((cells, planes * CAP), BF16),
            pltpu.VMEM((cells, planes * CAP), BF16),
            pltpu.VMEM((2, cells, width), F32),
            pltpu.VMEM((6, 2, cells, width), F32),
            pltpu.VMEM((7, 2, PAD, width), F32),
            pltpu.VMEM((7, PAD, width), F32),
            pltpu.VMEM((2, tall, width), F32),
            pltpu.VMEM((tall, width), F32),
            pltpu.VMEM((PAD, width), F32),
            pltpu.VMEM((deep, cells, width), F32),
            pltpu.VMEM((deep, PAD, width), F32),
            pltpu.VMEM((deep, PAD, width), F32),
            pltpu.VMEM((deep, cells, width), F32),
            pltpu.VMEM((deep, PAD, width), F32),
            pltpu.VMEM((2, deep, tall, width), F32),
            pltpu.VMEM((2, deep, tall, width), F32),
            pltpu.VMEM((2, 2, tall, width), F32),
            pltpu.VMEM((2, 5, deep, tall, width), F32),
            pltpu.VMEM((2, 1, width), F32),
            pltpu.VMEM((column, 1, width), F32),
            pltpu.VMEM((planes, 1, width), F32),
            pltpu.VMEM((1, width), F32),
            dma((9,)),
            dma((planes,)),
            dma((planes,)),
            dma,
            dma,
            dma((3,)),
            dma((6,)),
            dma((7,)),
            dma((7,)),
            dma((2,)),
            dma((2,)),
            dma((3,)),
            dma((3,)),
            dma((3,)),
            dma((3,)),
            dma((3,)),
            dma((3,)),
            dma((2,)),
            dma((4,)),
            dma,
            dma((column,)),
            dma((planes,)),
            dma((planes,)),
            dma((column,)),
            dma,
        ],
        compiler_params=pltpu.CompilerParams(collective_id=0, has_side_effects=True),
    )(*operands)
    along, across = coef[0], coef[1]
    solution_field = start_field + along * fields[1] - across * fields[3]
    residual = fields[0] - along * fields[2] + across * fields[4]
    return solution_field, residual


def solution(mesh):
    in_specs = (
        P("phi", "row"),
        P("phi"),
        P("phi"),
        P(None, "phi"),
        P("row", None),
        P(),
        P(),
        P(),
        P("row", "phi", None),
    )
    out_specs = (P("row", "phi", None), P("row", "phi", None))
    return jax.shard_map(body, mesh=mesh, in_specs=in_specs, out_specs=out_specs, check_vma=False)
```

```python
import functools

import jax
import jax.numpy as jnp
from jax import lax
from jax.experimental import pallas as pl
from jax.experimental.pallas import tpu as pltpu
from jax.sharding import PartitionSpec as P

MESH = pl.DeviceIdType.MESH
CAP = 8
PAD = 8
EDGE = 3
F32 = jnp.float32
BF16 = jnp.bfloat16


def roll(x, shift, axis):
    return pltpu.roll(x, shift % x.shape[axis], axis)


def kernel(
    phis,
    rows,
    mag_hbm,
    owner_hbm,
    offset_hbm,
    weight_hbm,
    theta_hbm,
    radial_hbm,
    theta_coef_hbm,
    phi_coef_hbm,
    start_hbm,
    fields_out,
    coef_out,
    mag_ref,
    owner_ref,
    offset_ref,
    weight_ref,
    theta_ref,
    radial_ref,
    theta_coef_ref,
    phi_coef_ref,
    pack,
    recv,
    wsend,
    wrecv,
    part,
    main,
    near_part,
    far_part,
    bound,
    forward,
    far_forward,
    mid,
    near_ghost,
    far_ghost,
    lend,
    lent,
    field,
    inverse,
    faces,
    values,
    sums,
    sums_column,
    sums_plane,
    totals,
    in_sem,
    pack_send,
    pack_recv,
    w_send,
    w_recv,
    part_send,
    main_recv,
    near_recv,
    far_recv,
    forward_send,
    forward_recv,
    radial_send,
    radial_recv,
    nghost_send,
    nghost_recv,
    fghost_send,
    fghost_recv,
    lend_send,
    lend_recv,
    column_send,
    column_recv,
    plane_send,
    plane_recv,
    total_send,
    total_recv,
):
    phi = lax.axis_index("phi")
    row = lax.axis_index("row")
    planes = phis // 2
    column = 2 * rows
    layers = start_hbm.shape[0]
    cells = start_hbm.shape[1]
    width = start_hbm.shape[2]
    tall = cells + 2 * PAD
    deep = layers + 2 * EDGE
    core = lax.rem(phi, 2)
    half = lax.rem(lax.div(phi, 2), 2)
    other = 1 - half
    here = lax.div(phi, 4) * 2 + core
    depth = half * rows + row
    slots = planes * 2 * CAP
    is_root = depth == 0
    is_second = depth == rows

    above = {1: 0, 2: 0, 3: 2, 4: 2, 5: 6, 6: 0, 7: 6, 8: 6}
    parents = {z: above[z] for z in range(1, rows)}
    parents.update({column - d: (column - above[d]) % column for d in range(1, rows + 1)})
    children = {z: [c for c in sorted(parents) if parents[c] == z] for z in range(column)}

    def table(entries):
        result = 0
        for z, entry in entries.items():
            if entry:
                result = jnp.where(depth == z, entry, result).astype(jnp.int32)
        return result

    parent_depth = table(parents)
    parent_half = jnp.where(parent_depth >= rows, 1, 0).astype(jnp.int32)
    parent_row = parent_depth - parent_half * rows
    tree_slot = table({z: children[p].index(z) for z, p in parents.items()})
    is_feeder = jnp.logical_and(parent_depth == 0, depth != 0)
    feeders = [(0, 0)] + [(z, 1 + slot) for slot, z in enumerate(children[0])]
    feeder_slot = jnp.where(is_feeder, 1 + tree_slot, 0).astype(jnp.int32)
    most = max(len(children[z]) for z in range(1, column))
    has_child = [
        table({z: len(children[z]) > index for z in range(1, column)}) > 0
        for index in range(most)
    ]
    child_row = [
        table(
            {
                z: children[z][index] % rows
                for z in range(1, column)
                if len(children[z]) > index
            }
        )
        for index in range(most)
    ]

    def phi_of(place, side):
        return lax.div(place, 2) * 4 + side * 2 + lax.rem(place, 2)

    def wrap(index):
        return lax.rem(index + phis, phis)

    def place_of(index):
        return lax.div(index, 4) * 2 + lax.rem(index, 2)

    twin = here + 1 - 2 * core
    near = phi + 1 - 2 * core
    far_step = 2 * core - 1
    far = wrap(phi + far_step)
    early_phi, late_phi = phi_of(here, 0), phi_of(here, 1)
    far_of_early, far_of_late = wrap(early_phi + far_step), wrap(late_phi + far_step)
    early_twin_phi = phi_of(twin, 0)
    last = cells - PAD
    near_src = pl.multiple_of((1 - core) * last, PAD)
    far_src = pl.multiple_of(core * last, PAD)

    has_next = row < rows - 1
    has_previous = row > 0

    def steps(act):
        act(0)

        @pl.when(has_next)
        def _():
            act(1)

        @pl.when(has_previous)
        def _():
            act(-1)

    barrier = pltpu.get_barrier_semaphore()

    def greet(device, level):
        pl.semaphore_signal(barrier, inc=1, device_id=(device, level), device_id_type=MESH)

    @pl.loop(1, planes)
    def _(step):
        greet(phi_of(lax.rem(here + step, planes), half), row)

    inputs = [
        pltpu.make_async_copy(src, dst, in_sem.at[index])
        for index, (src, dst) in enumerate(
            (
                (owner_hbm, owner_ref),
                (offset_hbm, offset_ref),
                (mag_hbm, mag_ref),
                (weight_hbm, weight_ref),
                (start_hbm, mid.at[EDGE : EDGE + layers]),
                (radial_hbm, radial_ref),
                (theta_coef_hbm, theta_coef_ref),
                (phi_coef_hbm, phi_coef_ref),
                (theta_hbm, theta_ref),
            )
        )
    ]
    for copy in inputs:
        copy.start()

    greet(phi_of(here, other), lax.rem(row + rows - rows // 2, rows))

    def greet_rows(step):
        if step != 0:
            greet(phi, row + step)
            greet(near, row + step)

    steps(greet_rows)

    @pl.when(half == 0)
    def _():
        greet(far, row)

    @pl.when(is_root)
    def _():
        for z, _slot in feeders:
            side, level = z // rows, z % rows
            greet(phi_of(twin, side), level)
            greet(phi_of(place_of(far_of_early), side), level)

        @pl.loop(1, column)
        def _(z):
            greet(phi_of(here, lax.div(z, rows)), lax.rem(z, rows))

    for index in range(most):

        @pl.when(has_child[index])
        def _():
            greet(phi, child_row[index])

    for index in range(3):
        inputs[index].wait()
    owner = owner_ref[...]
    target = (owner >> 2) * 32 + (owner & 1) * 16 + ((owner >> 1) & 1) * 8 + offset_ref[...]
    slot = lax.broadcasted_iota(jnp.int32, (slots, owner.shape[1]), 0)
    chosen = jnp.where(slot == target, 1.0, 0.0).astype(BF16)
    packed = jnp.dot(chosen, mag_ref[...], preferred_element_type=F32).astype(BF16)
    pack[...] = packed.reshape(planes, 2 * CAP, width)
    recv[here] = pack[here]

    inputs[3].wait()
    weights = weight_ref[...]
    from_slot = lax.broadcasted_iota(jnp.int32, (slots, planes * CAP), 0)
    to_slot = lax.broadcasted_iota(jnp.int32, (slots, planes * CAP), 1)
    source = to_slot >> 3
    natural = ((source >> 1) * 4 + other * 2 + (source & 1)) * CAP + (to_slot & 7)
    pick = jnp.where(from_slot == natural, 1.0, 0.0).astype(BF16)
    wsend[...] = jnp.dot(weights, pick, preferred_element_type=F32).astype(BF16)
    inputs[4].wait()

    def flag(condition):
        return jnp.where(condition, 1, 0).astype(jnp.int32)

    pl.semaphore_wait(
        barrier,
        (planes - 1)
        + 1
        + 2 * (flag(has_next) + flag(has_previous))
        + half
        + flag(depth != 0)
        + 2 * flag(jnp.logical_or(is_feeder, is_root))
        + flag(parent_depth != 0),
    )

    def remote(src, dst, send, receive, device, level):
        return pltpu.make_async_remote_copy(
            src_ref=src,
            dst_ref=dst,
            send_sem=send,
            recv_sem=receive,
            device_id=(device, level),
            device_id_type=MESH,
        )

    weight_copy = remote(
        wsend, wrecv, w_send, w_recv, phi_of(here, other), lax.rem(row + rows // 2, rows)
    )
    weight_copy.start()

    def layers_of(step):
        if step == 0:
            return pl.ds(EDGE, layers), pl.ds(EDGE, layers)
        if step > 0:
            return pl.ds(layers, EDGE), pl.ds(0, EDGE)
        return pl.ds(EDGE, EDGE), pl.ds(EDGE + layers, EDGE)

    def radial_copy(step):
        source, ghost = layers_of(step)
        return remote(
            mid.at[source],
            mid.at[ghost],
            radial_send.at[1 + step],
            radial_recv.at[1 - step],
            phi,
            row + step,
        )

    def near_copy(step):
        source, ghost = layers_of(step)
        return remote(
            mid.at[source, pl.ds(near_src, PAD)],
            near_ghost.at[ghost],
            nghost_send.at[1 + step],
            nghost_recv.at[1 - step],
            near,
            row + step,
        )

    def far_copy(step):
        source, ghost = layers_of(step)
        if step == 0:
            return remote(
                mid.at[source, pl.ds(far_src, PAD)],
                far_ghost.at[ghost],
                fghost_send.at[1],
                fghost_recv.at[1],
                far,
                row,
            )
        return remote(
            far_ghost.at[source],
            far_ghost.at[ghost],
            fghost_send.at[1 + step],
            fghost_recv.at[1 - step],
            phi,
            row + step,
        )

    def pass_far(step):
        if step == 0:
            arrival(far_ghost, fghost_recv, 0).wait_recv()
        else:
            far_copy(step).start()

    def wait_passed(step):
        if step != 0:
            arrival(far_ghost, fghost_recv, step).wait_recv()

    def arrival(buffer, semaphore, step):
        _, ghost = layers_of(-step)
        return remote(
            buffer.at[ghost], buffer.at[ghost], w_send, semaphore.at[1 + step], near, row
        )

    lend_copy = remote(
        lend,
        lent.at[:, pl.ds(PAD, cells)],
        lend_send,
        lend_recv,
        early_phi,
        0,
    )

    @pl.when(half == 1)
    def _():
        far_copy(0).start()

    def pack_copy(place, slot):
        return remote(
            pack.at[place],
            recv.at[slot],
            pack_send.at[place],
            pack_recv.at[slot],
            phi_of(place, half),
            row,
        )

    @pl.loop(1, planes)
    def _(step):
        pack_copy(lax.rem(here + step, planes), here).start()

    def row_copies(step):
        if step != 0:
            radial_copy(step).start()
        near_copy(step).start()

    steps(row_copies)

    for index in range(5, 9):
        inputs[index].wait()
    lanes = lax.broadcasted_iota(jnp.int32, (tall, width), 1)
    theta_coef = jnp.broadcast_to(theta_coef_ref[...], (tall, width))
    theta_upper = jnp.where(lanes < width - 1, 0.5 * (theta_coef + roll(theta_coef, -1, 1)), 0.0)
    theta_lower = jnp.where(lanes > 0, roll(theta_upper, 1, 1), 0.0)
    lines = phi_coef_ref.shape[0]
    lane8 = lax.broadcasted_iota(jnp.int32, (8, width), 1)
    top_index = layers * rows - 1

    def radial_faces(level):
        def coef_at(index):
            return radial_ref[jnp.clip(index, 0, top_index)]

        return [
            0.5
            * (
                coef_at(level * layers + i - EDGE - 1)
                + coef_at(level * layers + i - EDGE)
            )
            for i in range(deep + 1)
        ]

    def inside(level, i):
        index = level * layers + i - EDGE
        return jnp.logical_and(index >= 0, index <= top_index)

    def set_faces(which, slab, level):
        first = lax.rem(slab * cells - PAD + lines * width, lines * width)
        line = lax.div(first, width)
        shift = width - lax.rem(first, width)
        near_line = phi_coef_ref[pl.ds(line, 1), :]
        next_line = phi_coef_ref[pl.ds(lax.rem(line + 1, lines), 1), :]
        window = jnp.where(
            lane8 < shift,
            pltpu.roll(jnp.broadcast_to(near_line, (8, width)), shift, 1),
            pltpu.roll(jnp.broadcast_to(next_line, (8, width)), shift, 1),
        )
        phi_face = 0.5 * (window + roll(window, -1, 1))
        phi_upper = jnp.broadcast_to(phi_face[0:1], (width, width)).T[:tall]
        phi_lower = roll(phi_upper, 1, 0)
        faces[which, 0] = phi_upper
        faces[which, 1] = phi_lower
        radial = radial_faces(level)
        around = phi_upper + phi_lower + theta_upper + theta_lower
        for i in range(1, deep - 1):
            weight = jnp.where(inside(level, i), 1.0, 0.0).astype(F32)
            inverse[which, i] = weight / (radial[i] + radial[i + 1] + around)

    def image(which, radial, cell, i):
        phi_upper, phi_lower = faces[which, 0], faces[which, 1]
        value = cell(i)
        result = radial[i + 1] * (value - cell(i + 1))
        result = result + radial[i] * (value - cell(i - 1))
        result = result + theta_upper * (value - roll(value, -1, 1))
        result = result + theta_lower * (value - roll(value, 1, 1))
        result = result + phi_upper * (value - roll(value, -1, 0))
        return result + phi_lower * (value - roll(value, 1, 0))

    def at(which, kind):
        return lambda i: values[which, kind, i]

    def evaluate(which, level):
        radial = radial_faces(level)
        for i in range(1, deep - 1):
            residual = -image(which, radial, lambda j: field[which, j], i)
            values[which, 0, i] = residual
            values[which, 1, i] = residual * inverse[which, i]
        for i in range(2, deep - 2):
            first = image(which, radial, at(which, 1), i)
            values[which, 2, i] = first
            values[which, 3, i] = first * inverse[which, i]
        for i in range(3, deep - 3):
            values[which, 4, i] = image(which, radial, at(which, 3), i)

    def add_boundary(which, boundary):
        radial = radial_faces(0)
        residual = values[which, 0, EDGE] + radial[EDGE] * boundary
        values[which, 0, EDGE] = residual
        values[which, 1, EDGE] = residual * inverse[which, EDGE]
        for i in (EDGE, EDGE + 1):
            first = image(which, radial, at(which, 1), i)
            values[which, 2, i] = first
            values[which, 3, i] = first * inverse[which, i]
        for i in (EDGE, EDGE + 1, EDGE + 2):
            values[which, 4, i] = image(which, radial, at(which, 3), i)

    cell_index = lax.broadcasted_iota(jnp.int32, (tall, width), 0)
    lane = lax.broadcasted_iota(jnp.int32, (1, width), 1)

    def four_sums(terms, side):
        reach = EDGE * (1 - 2 * side)
        low = PAD - (1 - core) * reach
        high = PAD + cells + core * reach
        counted = jnp.logical_and(cell_index >= low, cell_index < high)
        result = jnp.zeros((1, width), F32)
        for index, total in enumerate(terms):
            total = jnp.where(counted, total, 0.0)
            total = jnp.sum(total, axis=0, keepdims=True)
            total = jnp.sum(total, axis=1, keepdims=True)
            result = jnp.where(lane == index, total, result)
        return result

    def inner_sums(which, side):
        terms = []
        for left, right in ((0, 1), (1, 2), (2, 3), (3, 4)):
            total = None
            for i in range(EDGE, EDGE + layers):
                product = values[which, left, i] * values[which, right, i]
                total = product if total is None else total + product
            terms.append(total)
        return four_sums(terms, side)

    def boundary_sums(which, boundary, fields, side):
        radial = radial_faces(0)
        zero = jnp.zeros_like(boundary)
        added = radial[EDGE] * boundary
        scaled = added * inverse[which, EDGE]

        def first(i):
            return scaled if i == EDGE else zero

        image0, image1 = (image(which, radial, first, EDGE + i) for i in (0, 1))
        image_scaled = (image0 * inverse[which, EDGE], image1 * inverse[which, EDGE + 1])

        def second(i):
            return image_scaled[i - EDGE] if i in (EDGE, EDGE + 1) else zero

        last0, last1 = (image(which, radial, second, EDGE + i) for i in (0, 1))
        return four_sums(
            (
                added * (2.0 * fields[0] + scaled),
                2.0 * added * fields[1] + scaled * image0,
                2.0 * scaled * fields[2] + image0 * image_scaled[0] + image1 * image_scaled[1],
                image_scaled[0] * (2.0 * fields[2] + last0)
                + image_scaled[1] * (2.0 * fields[3] + last1),
            ),
            side,
        )

    def assemble(which, middle, near_cells, far_cells, level):
        for i in range(deep):
            keep = inside(level, i)
            near_value = jnp.where(keep, near_cells[i], 0.0)
            far_value = jnp.zeros_like(near_value)
            if far_cells is not None:
                far_value = jnp.where(keep, far_cells[i], 0.0)
            field[which, i, 0:PAD] = jnp.where(core == 0, far_value, near_value)
            field[which, i, PAD + cells : tall] = jnp.where(core == 0, near_value, far_value)
            field[which, i, PAD : PAD + cells] = jnp.where(keep, middle[i], 0.0)

    set_faces(0, phi, row)
    column_copy = remote(
        sums.at[0], sums_column.at[depth], column_send, column_recv.at[depth], early_phi, 0
    )

    def wait_rows(step):
        if step != 0:
            arrival(mid, radial_recv, step).wait_recv()
        arrival(near_ghost, nghost_recv, step).wait_recv()

    def late_sums():
        steps(wait_rows)
        assemble(0, mid, near_ghost, None, row)
        evaluate(0, row)
        sums[0] = inner_sums(0, 1)
        column_copy.start()

    wide = (slots, slots)
    from_slot = lax.broadcasted_iota(jnp.int32, wide, 0)
    to_slot = lax.broadcasted_iota(jnp.int32, wide, 1)
    source = to_slot >> 4
    natural = ((source >> 1) * 4 + half * 2 + (source & 1)) * CAP + (to_slot & 7)
    mine = jnp.logical_and(from_slot == natural, ((to_slot >> 3) & 1) == half)
    own_weights = jnp.dot(
        weights, jnp.where(mine, 1.0, 0.0).astype(BF16), preferred_element_type=F32
    )
    from_slot = lax.broadcasted_iota(jnp.int32, (planes * CAP, slots), 0)
    to_slot = lax.broadcasted_iota(jnp.int32, (planes * CAP, slots), 1)
    theirs = jnp.logical_and(
        from_slot == (to_slot >> 4) * CAP + (to_slot & 7), ((to_slot >> 3) & 1) == other
    )
    theirs = jnp.where(theirs, 1.0, 0.0).astype(BF16)
    theta = theta_ref[...].astype(F32)
    weight_copy.wait_recv()
    partner_weights = jnp.dot(wrecv[...], theirs, preferred_element_type=F32)
    both_weights = jnp.concatenate(
        [
            jnp.where(half == 0, own_weights, partner_weights),
            jnp.where(half == 0, partner_weights, own_weights),
        ],
        axis=0,
    ).astype(BF16)

    @pl.loop(1, planes)
    def _(step):
        place = lax.rem(here + step, planes)
        pack_copy(place, place).wait_recv()

    columns = jnp.dot(
        both_weights, recv[...].reshape(slots, width), preferred_element_type=F32
    )
    product = jnp.dot(
        columns, theta, preferred_element_type=F32, precision=lax.Precision.HIGHEST
    )
    part[...] = product.reshape(2, cells, width)

    def child_copy(slot):
        return remote(part, main.at[slot], part_send.at[0], main_recv.at[slot], phi, row)

    main_copy = remote(
        part,
        main.at[tree_slot],
        part_send.at[0],
        main_recv.at[tree_slot],
        phi_of(here, parent_half),
        parent_row,
    )
    near_part_copy = remote(
        part.at[:, pl.ds(near_src, PAD)],
        near_part.at[feeder_slot],
        part_send.at[1],
        near_recv.at[feeder_slot],
        early_twin_phi,
        0,
    )
    far_part_copy = remote(
        part.at[1, pl.ds(far_src, PAD)],
        far_part.at[feeder_slot],
        part_send.at[2],
        far_recv.at[feeder_slot],
        far_of_late,
        0,
    )

    def send_part():
        @pl.when(depth != 0)
        def _():
            main_copy.start()

        @pl.when(jnp.logical_or(is_feeder, is_root))
        def _():
            far_part_copy.start()
            near_part_copy.start()

    is_leaf = jnp.logical_not(has_child[0]) if most else row >= 0

    @pl.when(is_leaf)
    def _():
        send_part()

    @pl.when(half == 0)
    def _():
        steps(pass_far)

    for index in range(most):

        @pl.when(has_child[index])
        def _():
            child_copy(index).wait_recv()
            part[...] += main[index]

    @pl.when(jnp.logical_not(is_leaf))
    def _():
        send_part()

    @pl.when(half == 1)
    def _():
        late_sums()

        @pl.when(is_second)
        def _():
            for index, (kind, i) in enumerate(((1, EDGE), (3, EDGE), (4, EDGE), (4, EDGE + 1))):
                lend[index] = values[0, kind, i, PAD : PAD + cells]
            lend_copy.start()

    @pl.when(half == 0)
    def _():
        steps(wait_rows)
        steps(wait_passed)
        assemble(0, mid, near_ghost, far_ghost, row)
        evaluate(0, row)

        sums[0] = inner_sums(0, 0)

        @pl.when(depth != 0)
        def _():
            column_copy.start()
            far_copy(0).start()

    def total_copy(z):
        return remote(
            totals,
            totals,
            total_send.at[z],
            total_recv,
            phi_of(here, lax.div(z, rows)),
            lax.rem(z, rows),
        )

    def plane_copy(place, slot):
        return remote(
            sums.at[1],
            sums_plane.at[slot],
            plane_send.at[place],
            plane_recv.at[slot],
            phi_of(place, 0),
            0,
        )

    forward_copy = remote(
        bound.at[1], forward, forward_send.at[0], forward_recv.at[0], late_phi, 0
    )
    far_forward_copy = remote(
        bound.at[0, pl.ds(pl.multiple_of(PAD + far_src, PAD), PAD)],
        far_forward,
        forward_send.at[1],
        forward_recv.at[1],
        far_of_early,
        0,
    )

    def keep_fields():
        for kind in range(5):
            for layer in range(layers):
                fields_out[kind, layer] = values[0, kind, EDGE + layer, PAD : PAD + cells]

    def sides(near_value, far_value):
        return (
            jnp.where(core == 0, far_value, near_value),
            jnp.where(core == 0, near_value, far_value),
        )

    @pl.when(is_root)
    def _():
        set_faces(1, late_phi, 0)
        lend_copy.wait_recv()

        @pl.loop(1, column)
        def _(z):
            remote(
                sums.at[0], sums_column.at[z], column_send, column_recv.at[z], phi, 0
            ).wait_recv()

        middle, nears, fars = part[...], None, None
        for _z, slot in feeders:
            remote(
                near_part.at[slot], near_part.at[slot], part_send.at[1], near_recv.at[slot], phi, 0
            ).wait_recv()
            remote(
                far_part.at[slot], far_part.at[slot], part_send.at[2], far_recv.at[slot], phi, 0
            ).wait_recv()
            nears = near_part[slot] if nears is None else nears + near_part[slot]
            fars = far_part[slot] if fars is None else fars + far_part[slot]
            if slot:
                child_copy(slot - 1).wait_recv()
                middle = middle + main[slot - 1]
        for which in (0, 1):
            low, high = sides(nears[which], fars if which == 0 else jnp.zeros_like(fars))
            bound[which, 0:PAD] = low
            bound[which, PAD : PAD + cells] = middle[which]
            bound[which, PAD + cells : tall] = high
        own_fields = (values[0, 1, EDGE], values[0, 3, EDGE], values[0, 4, EDGE], values[0, 4, EDGE + 1])
        sums_column[0] = (
            sums[0]
            + boundary_sums(0, bound[0], own_fields, 0)
            + boundary_sums(1, bound[1], [lent[index] for index in range(4)], 1)
        )
        mine = jnp.sum(sums_column[...], axis=0)
        sums[1] = mine
        sums_plane[here] = mine

        @pl.loop(1, planes)
        def _(step):
            plane_copy(lax.rem(here + step, planes), here).start()

        far_copy(0).start()
        forward_copy.start()
        far_forward_copy.start()
        add_boundary(0, bound[0])
        keep_fields()

        @pl.loop(1, planes)
        def _(step):
            place = lax.rem(here + step, planes)
            plane_copy(place, place).wait_recv()

        totals[...] = jnp.sum(sums_plane[...], axis=0)

        @pl.loop(1, column)
        def _(z):
            total_copy(z).start()

    @pl.when(half == 1)
    def _():
        steps(pass_far)
        steps(wait_passed)
        assemble(0, mid, near_ghost, far_ghost, row)
        evaluate(0, row)

    @pl.when(is_second)
    def _():
        forward_copy.wait_recv()
        far_forward_copy.wait_recv()
        boundary = forward[...]
        edge = jnp.where(core == 0, far_forward[...], boundary[0:PAD])
        other_edge = jnp.where(core == 0, boundary[PAD + cells :], far_forward[...])
        add_boundary(
            0, jnp.concatenate([edge, boundary[PAD : PAD + cells], other_edge], axis=0)
        )

    @pl.when(depth != 0)
    def _():
        keep_fields()
        remote(totals, totals, total_send.at[0], total_recv, phi, 0).wait_recv()

    total = totals[...]
    rz, pq, qw, wt = (
        jnp.sum(jnp.where(lane == index, total, 0.0), axis=1, keepdims=True)
        for index in range(4)
    )
    step0 = rz / pq
    rz_next = step0 * step0 * qw - rz
    ratio = 1.0 + rz_next / rz
    step1 = rz_next / (step0 * step0 * wt - ratio * ratio * pq)
    along = step0 + step1 * ratio
    across = step0 * step1
    coef_out[0:1] = jnp.broadcast_to(along, (1, width))
    coef_out[1:2] = jnp.broadcast_to(across, (1, width))

    weight_copy.wait_send()

    @pl.loop(1, planes)
    def _(step):
        pack_copy(lax.rem(here + step, planes), here).wait_send()

    def sent_rows(step):
        if step != 0:
            radial_copy(step).wait_send()
        near_copy(step).wait_send()
        far_copy(step).wait_send()

    steps(sent_rows)

    @pl.when(is_second)
    def _():
        lend_copy.wait_send()


    @pl.when(jnp.logical_or(is_feeder, is_root))
    def _():
        near_part_copy.wait_send()
        far_part_copy.wait_send()

    @pl.when(depth != 0)
    def _():
        main_copy.wait_send()
        column_copy.wait_send()

    @pl.when(is_root)
    def _():
        forward_copy.wait_send()
        far_forward_copy.wait_send()

        @pl.loop(1, planes)
        def _(step):
            plane_copy(lax.rem(here + step, planes), here).wait_send()

        @pl.loop(1, column)
        def _(z):
            total_copy(z).wait_send()


def body(
    magnetogram,
    col_owner,
    col_offset,
    phi_weight,
    theta_weight,
    radial_coef,
    theta_coef,
    phi_coef,
    start_field,
):
    phis, rows = lax.axis_size("phi"), lax.axis_size("row")
    layers, cells, width = start_field.shape
    planes, column = phis // 2, 2 * rows
    slots = phis * CAP
    tall = cells + 2 * PAD
    deep = layers + 2 * EDGE
    dma = pltpu.SemaphoreType.DMA
    anywhere = pl.BlockSpec(memory_space=pl.ANY)
    operands = (
        magnetogram,
        col_owner.reshape(1, -1),
        col_offset.reshape(1, -1),
        phi_weight.T,
        theta_weight,
        radial_coef,
        theta_coef.reshape(1, -1),
        phi_coef.reshape(-1, width),
        start_field,
    )
    local = [pltpu.VMEM(x.shape, x.dtype) for x in operands[:8]]
    local[5] = pltpu.SMEM(radial_coef.shape, F32)
    fields, coef = pl.pallas_call(
        functools.partial(kernel, phis, rows),
        out_shape=(
            pltpu.VMEM((5,) + start_field.shape, F32),
            pltpu.VMEM((2, width), F32),
        ),
        in_specs=[anywhere] * 9,
        out_specs=(pl.BlockSpec(memory_space=pltpu.VMEM),) * 2,
        scratch_shapes=local
        + [
            pltpu.VMEM((planes, 2 * CAP, width), BF16),
            pltpu.VMEM((planes, 2 * CAP, width), BF16),
            pltpu.VMEM((cells, planes * CAP), BF16),
            pltpu.VMEM((cells, planes * CAP), BF16),
            pltpu.VMEM((2, cells, width), F32),
            pltpu.VMEM((6, 2, cells, width), F32),
            pltpu.VMEM((7, 2, PAD, width), F32),
            pltpu.VMEM((7, PAD, width), F32),
            pltpu.VMEM((2, tall, width), F32),
            pltpu.VMEM((tall, width), F32),
            pltpu.VMEM((PAD, width), F32),
            pltpu.VMEM((deep, cells, width), F32),
            pltpu.VMEM((deep, PAD, width), F32),
            pltpu.VMEM((deep, PAD, width), F32),
            pltpu.VMEM((4, cells, width), F32),
            pltpu.VMEM((4, tall, width), F32),
            pltpu.VMEM((1, deep, tall, width), F32),
            pltpu.VMEM((2, deep, tall, width), F32),
            pltpu.VMEM((2, 2, tall, width), F32),
            pltpu.VMEM((1, 5, deep, tall, width), F32),
            pltpu.VMEM((2, 1, width), F32),
            pltpu.VMEM((column, 1, width), F32),
            pltpu.VMEM((planes, 1, width), F32),
            pltpu.VMEM((1, width), F32),
            dma((9,)),
            dma((planes,)),
            dma((planes,)),
            dma,
            dma,
            dma((3,)),
            dma((6,)),
            dma((7,)),
            dma((7,)),
            dma((2,)),
            dma((2,)),
            dma((3,)),
            dma((3,)),
            dma((3,)),
            dma((3,)),
            dma((3,)),
            dma((3,)),
            dma,
            dma,
            dma,
            dma((column,)),
            dma((planes,)),
            dma((planes,)),
            dma((column,)),
            dma,
        ],
        compiler_params=pltpu.CompilerParams(collective_id=0, has_side_effects=True),
    )(*operands)
    along, across = coef[0], coef[1]
    solution_field = start_field + along * fields[1] - across * fields[3]
    residual = fields[0] - along * fields[2] + across * fields[4]
    return solution_field, residual


def solution(mesh):
    in_specs = (
        P("phi", "row"),
        P("phi"),
        P("phi"),
        P(None, "phi"),
        P("row", None),
        P(),
        P(),
        P(),
        P("row", "phi", None),
    )
    out_specs = (P("row", "phi", None), P("row", "phi", None))
    return jax.shard_map(body, mesh=mesh, in_specs=in_specs, out_specs=out_specs, check_vma=False)
```

```python
import functools

import jax
import jax.numpy as jnp
from jax import lax
from jax.experimental import pallas as pl
from jax.experimental.pallas import tpu as pltpu
from jax.sharding import PartitionSpec as P

MESH = pl.DeviceIdType.MESH
CAP = 8
PAD = 8
EDGE = 3
F32 = jnp.float32
BF16 = jnp.bfloat16


def roll(x, shift, axis):
    return pltpu.roll(x, shift % x.shape[axis], axis)


def kernel(
    phis,
    rows,
    mag_hbm,
    owner_hbm,
    offset_hbm,
    weight_hbm,
    theta_hbm,
    radial_hbm,
    theta_coef_hbm,
    phi_coef_hbm,
    start_hbm,
    fields_out,
    coef_out,
    mag_ref,
    owner_ref,
    offset_ref,
    weight_ref,
    theta_ref,
    radial_ref,
    theta_coef_ref,
    phi_coef_ref,
    pack,
    recv,
    wsend,
    wrecv,
    part,
    main,
    near_part,
    far_part,
    bound,
    forward,
    far_forward,
    mid,
    near_ghost,
    far_ghost,
    lend,
    lent,
    field,
    inverse,
    faces,
    values,
    sums,
    sums_column,
    sums_plane,
    totals,
    in_sem,
    pack_send,
    pack_recv,
    w_send,
    w_recv,
    part_send,
    main_recv,
    near_recv,
    far_recv,
    forward_send,
    forward_recv,
    radial_send,
    radial_recv,
    nghost_send,
    nghost_recv,
    fghost_send,
    fghost_recv,
    lend_send,
    lend_recv,
    column_send,
    column_recv,
    plane_send,
    plane_recv,
    total_send,
    total_recv,
):
    phi = lax.axis_index("phi")
    row = lax.axis_index("row")
    planes = phis // 2
    column = 2 * rows
    layers = start_hbm.shape[0]
    cells = start_hbm.shape[1]
    width = start_hbm.shape[2]
    tall = cells + 2 * PAD
    deep = layers + 2 * EDGE
    core = lax.rem(phi, 2)
    half = lax.rem(lax.div(phi, 2), 2)
    other = 1 - half
    here = lax.div(phi, 4) * 2 + core
    depth = half * rows + row
    slots = planes * 2 * CAP
    is_root = depth == 0
    is_second = depth == rows

    above = {1: 0, 2: 0, 3: 2, 4: 2, 5: 6, 6: 0, 7: 6, 8: 6}
    parents = {z: above[z] for z in range(1, rows)}
    parents.update({column - d: (column - above[d]) % column for d in range(1, rows + 1)})
    children = {z: [c for c in sorted(parents) if parents[c] == z] for z in range(column)}

    def table(entries):
        result = 0
        for z, entry in entries.items():
            if entry:
                result = jnp.where(depth == z, entry, result).astype(jnp.int32)
        return result

    parent_depth = table(parents)
    parent_half = jnp.where(parent_depth >= rows, 1, 0).astype(jnp.int32)
    parent_row = parent_depth - parent_half * rows
    tree_slot = table({z: children[p].index(z) for z, p in parents.items()})
    is_feeder = jnp.logical_and(parent_depth == 0, depth != 0)
    feeders = [(0, 0)] + [(z, 1 + slot) for slot, z in enumerate(children[0])]
    feeder_slot = jnp.where(is_feeder, 1 + tree_slot, 0).astype(jnp.int32)
    most = max(len(children[z]) for z in range(1, column))
    has_child = [
        table({z: len(children[z]) > index for z in range(1, column)}) > 0
        for index in range(most)
    ]
    child_row = [
        table(
            {
                z: children[z][index] % rows
                for z in range(1, column)
                if len(children[z]) > index
            }
        )
        for index in range(most)
    ]

    def phi_of(place, side):
        return lax.div(place, 2) * 4 + side * 2 + lax.rem(place, 2)

    def wrap(index):
        return lax.rem(index + phis, phis)

    def place_of(index):
        return lax.div(index, 4) * 2 + lax.rem(index, 2)

    twin = here + 1 - 2 * core
    near = phi + 1 - 2 * core
    far_step = 2 * core - 1
    far = wrap(phi + far_step)
    early_phi, late_phi = phi_of(here, 0), phi_of(here, 1)
    far_of_early, far_of_late = wrap(early_phi + far_step), wrap(late_phi + far_step)
    early_twin_phi = phi_of(twin, 0)
    last = cells - PAD
    near_src = pl.multiple_of((1 - core) * last, PAD)
    far_src = pl.multiple_of(core * last, PAD)

    has_next = row < rows - 1
    has_previous = row > 0

    def steps(act):
        act(0)

        @pl.when(has_next)
        def _():
            act(1)

        @pl.when(has_previous)
        def _():
            act(-1)

    barrier = pltpu.get_barrier_semaphore()

    def greet(device, level):
        pl.semaphore_signal(barrier, inc=1, device_id=(device, level), device_id_type=MESH)

    @pl.loop(1, planes)
    def _(step):
        greet(phi_of(lax.rem(here + step, planes), half), row)

    inputs = [
        pltpu.make_async_copy(src, dst, in_sem.at[index])
        for index, (src, dst) in enumerate(
            (
                (owner_hbm, owner_ref),
                (offset_hbm, offset_ref),
                (mag_hbm, mag_ref),
                (weight_hbm, weight_ref),
                (start_hbm, mid.at[EDGE : EDGE + layers]),
                (radial_hbm, radial_ref),
                (theta_coef_hbm, theta_coef_ref),
                (phi_coef_hbm, phi_coef_ref),
                (theta_hbm, theta_ref),
            )
        )
    ]
    for copy in inputs:
        copy.start()

    greet(phi_of(here, other), lax.rem(row + rows - rows // 2, rows))

    def greet_rows(step):
        if step != 0:
            greet(phi, row + step)
            greet(near, row + step)

    steps(greet_rows)

    @pl.when(half == 0)
    def _():
        greet(far, row)

    @pl.when(is_root)
    def _():
        for z, _slot in feeders:
            side, level = z // rows, z % rows
            greet(phi_of(twin, side), level)
            greet(phi_of(place_of(far_of_early), side), level)

        @pl.loop(1, column)
        def _(z):
            greet(phi_of(here, lax.div(z, rows)), lax.rem(z, rows))

    for index in range(most):

        @pl.when(has_child[index])
        def _():
            greet(phi, child_row[index])

    for index in range(3):
        inputs[index].wait()
    owner = owner_ref[...]
    target = (owner >> 2) * 32 + (owner & 1) * 16 + ((owner >> 1) & 1) * 8 + offset_ref[...]
    slot = lax.broadcasted_iota(jnp.int32, (slots, owner.shape[1]), 0)
    chosen = jnp.where(slot == target, 1.0, 0.0).astype(BF16)
    packed = jnp.dot(chosen, mag_ref[...], preferred_element_type=F32).astype(BF16)
    pack[...] = packed.reshape(planes, 2 * CAP, width)
    recv[here] = pack[here]

    inputs[3].wait()
    weights = weight_ref[...]
    from_slot = lax.broadcasted_iota(jnp.int32, (slots, planes * CAP), 0)
    to_slot = lax.broadcasted_iota(jnp.int32, (slots, planes * CAP), 1)
    source = to_slot >> 3
    natural = ((source >> 1) * 4 + other * 2 + (source & 1)) * CAP + (to_slot & 7)
    pick = jnp.where(from_slot == natural, 1.0, 0.0).astype(BF16)
    wsend[...] = jnp.dot(weights, pick, preferred_element_type=F32).astype(BF16)
    inputs[4].wait()

    def flag(condition):
        return jnp.where(condition, 1, 0).astype(jnp.int32)

    pl.semaphore_wait(
        barrier,
        (planes - 1)
        + 1
        + 2 * (flag(has_next) + flag(has_previous))
        + half
        + flag(depth != 0)
        + 2 * flag(jnp.logical_or(is_feeder, is_root))
        + flag(parent_depth != 0),
    )

    def remote(src, dst, send, receive, device, level):
        return pltpu.make_async_remote_copy(
            src_ref=src,
            dst_ref=dst,
            send_sem=send,
            recv_sem=receive,
            device_id=(device, level),
            device_id_type=MESH,
        )

    weight_copy = remote(
        wsend, wrecv, w_send, w_recv, phi_of(here, other), lax.rem(row + rows // 2, rows)
    )

    def layers_of(step):
        if step == 0:
            return pl.ds(EDGE, layers), pl.ds(EDGE, layers)
        if step > 0:
            return pl.ds(layers, EDGE), pl.ds(0, EDGE)
        return pl.ds(EDGE, EDGE), pl.ds(EDGE + layers, EDGE)

    def radial_copy(step):
        source, ghost = layers_of(step)
        return remote(
            mid.at[source],
            mid.at[ghost],
            radial_send.at[1 + step],
            radial_recv.at[1 - step],
            phi,
            row + step,
        )

    def near_copy(step):
        source, ghost = layers_of(step)
        return remote(
            mid.at[source, pl.ds(near_src, PAD)],
            near_ghost.at[ghost],
            nghost_send.at[1 + step],
            nghost_recv.at[1 - step],
            near,
            row + step,
        )

    def far_copy(step):
        source, ghost = layers_of(step)
        if step == 0:
            return remote(
                mid.at[source, pl.ds(far_src, PAD)],
                far_ghost.at[ghost],
                fghost_send.at[1],
                fghost_recv.at[1],
                far,
                row,
            )
        return remote(
            far_ghost.at[source],
            far_ghost.at[ghost],
            fghost_send.at[1 + step],
            fghost_recv.at[1 - step],
            phi,
            row + step,
        )

    def pass_far(step):
        if step == 0:
            arrival(far_ghost, fghost_recv, 0).wait_recv()
        else:
            far_copy(step).start()

    def wait_passed(step):
        if step != 0:
            arrival(far_ghost, fghost_recv, step).wait_recv()

    def arrival(buffer, semaphore, step):
        _, ghost = layers_of(-step)
        return remote(
            buffer.at[ghost], buffer.at[ghost], w_send, semaphore.at[1 + step], near, row
        )

    lend_copy = remote(
        lend,
        lent.at[:, pl.ds(PAD, cells)],
        lend_send,
        lend_recv,
        early_phi,
        0,
    )

    @pl.when(half == 1)
    def _():
        far_copy(0).start()

    weight_copy.start()

    def pack_copy(place, slot):
        return remote(
            pack.at[place],
            recv.at[slot],
            pack_send.at[place],
            pack_recv.at[slot],
            phi_of(place, half),
            row,
        )

    @pl.loop(1, planes)
    def _(step):
        pack_copy(lax.rem(here + step, planes), here).start()

    def row_copies(step):
        if step != 0:
            radial_copy(step).start()
        near_copy(step).start()

    steps(row_copies)

    for index in range(5, 9):
        inputs[index].wait()
    lanes = lax.broadcasted_iota(jnp.int32, (tall, width), 1)
    theta_coef = jnp.broadcast_to(theta_coef_ref[...], (tall, width))
    theta_upper = jnp.where(lanes < width - 1, 0.5 * (theta_coef + roll(theta_coef, -1, 1)), 0.0)
    theta_lower = jnp.where(lanes > 0, roll(theta_upper, 1, 1), 0.0)
    lines = phi_coef_ref.shape[0]
    lane8 = lax.broadcasted_iota(jnp.int32, (8, width), 1)
    top_index = layers * rows - 1

    def radial_faces(level):
        def coef_at(index):
            return radial_ref[jnp.clip(index, 0, top_index)]

        return [
            0.5
            * (
                coef_at(level * layers + i - EDGE - 1)
                + coef_at(level * layers + i - EDGE)
            )
            for i in range(deep + 1)
        ]

    def inside(level, i):
        index = level * layers + i - EDGE
        return jnp.logical_and(index >= 0, index <= top_index)

    def set_faces(which, slab, level):
        first = lax.rem(slab * cells - PAD + lines * width, lines * width)
        line = lax.div(first, width)
        shift = width - lax.rem(first, width)
        near_line = phi_coef_ref[pl.ds(line, 1), :]
        next_line = phi_coef_ref[pl.ds(lax.rem(line + 1, lines), 1), :]
        window = jnp.where(
            lane8 < shift,
            pltpu.roll(jnp.broadcast_to(near_line, (8, width)), shift, 1),
            pltpu.roll(jnp.broadcast_to(next_line, (8, width)), shift, 1),
        )
        phi_face = 0.5 * (window + roll(window, -1, 1))
        phi_upper = jnp.broadcast_to(phi_face[0:1], (width, width)).T[:tall]
        phi_lower = roll(phi_upper, 1, 0)
        faces[which, 0] = phi_upper
        faces[which, 1] = phi_lower
        radial = radial_faces(level)
        around = phi_upper + phi_lower + theta_upper + theta_lower
        for i in range(1, deep - 1):
            weight = jnp.where(inside(level, i), 1.0, 0.0).astype(F32)
            inverse[which, i] = weight / (radial[i] + radial[i + 1] + around)

    def image(which, radial, cell, i):
        phi_upper, phi_lower = faces[which, 0], faces[which, 1]
        value = cell(i)
        result = radial[i + 1] * (value - cell(i + 1))
        result = result + radial[i] * (value - cell(i - 1))
        result = result + theta_upper * (value - roll(value, -1, 1))
        result = result + theta_lower * (value - roll(value, 1, 1))
        result = result + phi_upper * (value - roll(value, -1, 0))
        return result + phi_lower * (value - roll(value, 1, 0))

    def at(which, kind):
        return lambda i: values[which, kind, i]

    def evaluate(which, level):
        radial = radial_faces(level)
        for i in range(1, deep - 1):
            residual = -image(which, radial, lambda j: field[which, j], i)
            values[which, 0, i] = residual
            values[which, 1, i] = residual * inverse[which, i]
        for i in range(2, deep - 2):
            first = image(which, radial, at(which, 1), i)
            values[which, 2, i] = first
            values[which, 3, i] = first * inverse[which, i]
        for i in range(3, deep - 3):
            values[which, 4, i] = image(which, radial, at(which, 3), i)

    def add_boundary(which, boundary):
        radial = radial_faces(0)
        residual = values[which, 0, EDGE] + radial[EDGE] * boundary
        values[which, 0, EDGE] = residual
        values[which, 1, EDGE] = residual * inverse[which, EDGE]
        for i in (EDGE, EDGE + 1):
            first = image(which, radial, at(which, 1), i)
            values[which, 2, i] = first
            values[which, 3, i] = first * inverse[which, i]
        for i in (EDGE, EDGE + 1, EDGE + 2):
            values[which, 4, i] = image(which, radial, at(which, 3), i)

    cell_index = lax.broadcasted_iota(jnp.int32, (tall, width), 0)
    lane = lax.broadcasted_iota(jnp.int32, (1, width), 1)

    def four_sums(terms, side):
        reach = EDGE * (1 - 2 * side)
        low = PAD - (1 - core) * reach
        high = PAD + cells + core * reach
        counted = jnp.logical_and(cell_index >= low, cell_index < high)
        result = jnp.zeros((1, width), F32)
        for index, total in enumerate(terms):
            total = jnp.where(counted, total, 0.0)
            total = jnp.sum(total, axis=0, keepdims=True)
            total = jnp.sum(total, axis=1, keepdims=True)
            result = jnp.where(lane == index, total, result)
        return result

    def inner_sums(which, side):
        terms = []
        for left, right in ((0, 1), (1, 2), (2, 3), (3, 4)):
            total = None
            for i in range(EDGE, EDGE + layers):
                product = values[which, left, i] * values[which, right, i]
                total = product if total is None else total + product
            terms.append(total)
        return four_sums(terms, side)

    def boundary_sums(which, boundary, fields, side):
        radial = radial_faces(0)
        zero = jnp.zeros_like(boundary)
        added = radial[EDGE] * boundary
        scaled = added * inverse[which, EDGE]

        def first(i):
            return scaled if i == EDGE else zero

        image0, image1 = (image(which, radial, first, EDGE + i) for i in (0, 1))
        image_scaled = (image0 * inverse[which, EDGE], image1 * inverse[which, EDGE + 1])

        def second(i):
            return image_scaled[i - EDGE] if i in (EDGE, EDGE + 1) else zero

        last0, last1 = (image(which, radial, second, EDGE + i) for i in (0, 1))
        return four_sums(
            (
                added * (2.0 * fields[0] + scaled),
                2.0 * added * fields[1] + scaled * image0,
                2.0 * scaled * fields[2] + image0 * image_scaled[0] + image1 * image_scaled[1],
                image_scaled[0] * (2.0 * fields[2] + last0)
                + image_scaled[1] * (2.0 * fields[3] + last1),
            ),
            side,
        )

    def assemble(which, middle, near_cells, far_cells, level):
        for i in range(deep):
            keep = inside(level, i)
            near_value = jnp.where(keep, near_cells[i], 0.0)
            far_value = jnp.zeros_like(near_value)
            if far_cells is not None:
                far_value = jnp.where(keep, far_cells[i], 0.0)
            field[which, i, 0:PAD] = jnp.where(core == 0, far_value, near_value)
            field[which, i, PAD + cells : tall] = jnp.where(core == 0, near_value, far_value)
            field[which, i, PAD : PAD + cells] = jnp.where(keep, middle[i], 0.0)

    set_faces(0, phi, row)
    column_copy = remote(
        sums.at[0], sums_column.at[depth], column_send, column_recv.at[depth], early_phi, 0
    )

    def wait_rows(step):
        if step != 0:
            arrival(mid, radial_recv, step).wait_recv()
        arrival(near_ghost, nghost_recv, step).wait_recv()

    def late_sums():
        steps(wait_rows)
        assemble(0, mid, near_ghost, None, row)
        evaluate(0, row)
        sums[0] = inner_sums(0, 1)
        column_copy.start()

    wide = (slots, slots)
    from_slot = lax.broadcasted_iota(jnp.int32, wide, 0)
    to_slot = lax.broadcasted_iota(jnp.int32, wide, 1)
    source = to_slot >> 4
    natural = ((source >> 1) * 4 + half * 2 + (source & 1)) * CAP + (to_slot & 7)
    mine = jnp.logical_and(from_slot == natural, ((to_slot >> 3) & 1) == half)
    own_weights = jnp.dot(
        weights, jnp.where(mine, 1.0, 0.0).astype(BF16), preferred_element_type=F32
    )
    from_slot = lax.broadcasted_iota(jnp.int32, (planes * CAP, slots), 0)
    to_slot = lax.broadcasted_iota(jnp.int32, (planes * CAP, slots), 1)
    theirs = jnp.logical_and(
        from_slot == (to_slot >> 4) * CAP + (to_slot & 7), ((to_slot >> 3) & 1) == other
    )
    theirs = jnp.where(theirs, 1.0, 0.0).astype(BF16)
    theta = theta_ref[...].astype(F32)
    weight_copy.wait_recv()
    partner_weights = jnp.dot(wrecv[...], theirs, preferred_element_type=F32)
    both_weights = jnp.concatenate(
        [
            jnp.where(half == 0, own_weights, partner_weights),
            jnp.where(half == 0, partner_weights, own_weights),
        ],
        axis=0,
    ).astype(BF16)

    @pl.loop(1, planes)
    def _(step):
        place = lax.rem(here + step, planes)
        pack_copy(place, place).wait_recv()

    columns = jnp.dot(
        both_weights, recv[...].reshape(slots, width), preferred_element_type=F32
    )
    product = jnp.dot(
        columns, theta, preferred_element_type=F32, precision=lax.Precision.HIGHEST
    )
    part[...] = product.reshape(2, cells, width)

    def child_copy(slot):
        return remote(part, main.at[slot], part_send.at[0], main_recv.at[slot], phi, row)

    main_copy = remote(
        part,
        main.at[tree_slot],
        part_send.at[0],
        main_recv.at[tree_slot],
        phi_of(here, parent_half),
        parent_row,
    )
    near_part_copy = remote(
        part.at[:, pl.ds(near_src, PAD)],
        near_part.at[feeder_slot],
        part_send.at[1],
        near_recv.at[feeder_slot],
        early_twin_phi,
        0,
    )
    far_part_copy = remote(
        part.at[1, pl.ds(far_src, PAD)],
        far_part.at[feeder_slot],
        part_send.at[2],
        far_recv.at[feeder_slot],
        far_of_late,
        0,
    )

    def send_part():
        @pl.when(depth != 0)
        def _():
            main_copy.start()

        @pl.when(jnp.logical_or(is_feeder, is_root))
        def _():
            far_part_copy.start()
            near_part_copy.start()

    is_leaf = jnp.logical_not(has_child[0]) if most else row >= 0

    @pl.when(is_leaf)
    def _():
        send_part()

    @pl.when(half == 0)
    def _():
        steps(pass_far)

    for index in range(most):

        @pl.when(has_child[index])
        def _():
            child_copy(index).wait_recv()
            part[...] += main[index]

    @pl.when(jnp.logical_not(is_leaf))
    def _():
        send_part()

    @pl.when(half == 1)
    def _():
        late_sums()

        @pl.when(is_second)
        def _():
            for index, (kind, i) in enumerate(((1, EDGE), (3, EDGE), (4, EDGE), (4, EDGE + 1))):
                lend[index] = values[0, kind, i, PAD : PAD + cells]
            lend_copy.start()

    @pl.when(half == 0)
    def _():
        steps(wait_rows)
        steps(wait_passed)
        assemble(0, mid, near_ghost, far_ghost, row)
        evaluate(0, row)

        sums[0] = inner_sums(0, 0)

        @pl.when(depth != 0)
        def _():
            column_copy.start()
            far_copy(0).start()

    def total_copy(z):
        return remote(
            totals,
            totals,
            total_send.at[z],
            total_recv,
            phi_of(here, lax.div(z, rows)),
            lax.rem(z, rows),
        )

    def plane_copy(place, slot):
        return remote(
            sums.at[1],
            sums_plane.at[slot],
            plane_send.at[place],
            plane_recv.at[slot],
            phi_of(place, 0),
            0,
        )

    forward_copy = remote(
        bound.at[1], forward, forward_send.at[0], forward_recv.at[0], late_phi, 0
    )
    far_forward_copy = remote(
        bound.at[0, pl.ds(pl.multiple_of(PAD + far_src, PAD), PAD)],
        far_forward,
        forward_send.at[1],
        forward_recv.at[1],
        far_of_early,
        0,
    )

    def keep_fields():
        for kind in range(5):
            for layer in range(layers):
                fields_out[kind, layer] = values[0, kind, EDGE + layer, PAD : PAD + cells]

    def sides(near_value, far_value):
        return (
            jnp.where(core == 0, far_value, near_value),
            jnp.where(core == 0, near_value, far_value),
        )

    @pl.when(is_root)
    def _():
        set_faces(1, late_phi, 0)
        lend_copy.wait_recv()

        @pl.loop(1, column)
        def _(z):
            remote(
                sums.at[0], sums_column.at[z], column_send, column_recv.at[z], phi, 0
            ).wait_recv()

        middle, nears, fars = part[...], None, None
        for _z, slot in feeders:
            remote(
                near_part.at[slot], near_part.at[slot], part_send.at[1], near_recv.at[slot], phi, 0
            ).wait_recv()
            remote(
                far_part.at[slot], far_part.at[slot], part_send.at[2], far_recv.at[slot], phi, 0
            ).wait_recv()
            nears = near_part[slot] if nears is None else nears + near_part[slot]
            fars = far_part[slot] if fars is None else fars + far_part[slot]
            if slot:
                child_copy(slot - 1).wait_recv()
                middle = middle + main[slot - 1]
        for which in (0, 1):
            low, high = sides(nears[which], fars if which == 0 else jnp.zeros_like(fars))
            bound[which, 0:PAD] = low
            bound[which, PAD : PAD + cells] = middle[which]
            bound[which, PAD + cells : tall] = high
        own_fields = (values[0, 1, EDGE], values[0, 3, EDGE], values[0, 4, EDGE], values[0, 4, EDGE + 1])
        sums_column[0] = (
            sums[0]
            + boundary_sums(0, bound[0], own_fields, 0)
            + boundary_sums(1, bound[1], [lent[index] for index in range(4)], 1)
        )
        mine = jnp.sum(sums_column[...], axis=0)
        sums[1] = mine
        sums_plane[here] = mine

        @pl.loop(1, planes)
        def _(step):
            plane_copy(lax.rem(here + step, planes), here).start()

        far_copy(0).start()
        forward_copy.start()
        far_forward_copy.start()
        add_boundary(0, bound[0])
        keep_fields()

        @pl.loop(1, planes)
        def _(step):
            place = lax.rem(here + step, planes)
            plane_copy(place, place).wait_recv()

        totals[...] = jnp.sum(sums_plane[...], axis=0)

        @pl.loop(1, column)
        def _(z):
            total_copy(z).start()

    @pl.when(half == 1)
    def _():
        steps(pass_far)
        steps(wait_passed)
        assemble(0, mid, near_ghost, far_ghost, row)
        evaluate(0, row)

    @pl.when(is_second)
    def _():
        forward_copy.wait_recv()
        far_forward_copy.wait_recv()
        boundary = forward[...]
        edge = jnp.where(core == 0, far_forward[...], boundary[0:PAD])
        other_edge = jnp.where(core == 0, boundary[PAD + cells :], far_forward[...])
        add_boundary(
            0, jnp.concatenate([edge, boundary[PAD : PAD + cells], other_edge], axis=0)
        )

    @pl.when(depth != 0)
    def _():
        keep_fields()
        remote(totals, totals, total_send.at[0], total_recv, phi, 0).wait_recv()

    total = totals[...]
    rz, pq, qw, wt = (
        jnp.sum(jnp.where(lane == index, total, 0.0), axis=1, keepdims=True)
        for index in range(4)
    )
    step0 = rz / pq
    rz_next = step0 * step0 * qw - rz
    ratio = 1.0 + rz_next / rz
    step1 = rz_next / (step0 * step0 * wt - ratio * ratio * pq)
    along = step0 + step1 * ratio
    across = step0 * step1
    coef_out[0:1] = jnp.broadcast_to(along, (1, width))
    coef_out[1:2] = jnp.broadcast_to(across, (1, width))

    weight_copy.wait_send()

    @pl.loop(1, planes)
    def _(step):
        pack_copy(lax.rem(here + step, planes), here).wait_send()

    def sent_rows(step):
        if step != 0:
            radial_copy(step).wait_send()
        near_copy(step).wait_send()
        far_copy(step).wait_send()

    steps(sent_rows)

    @pl.when(is_second)
    def _():
        lend_copy.wait_send()


    @pl.when(jnp.logical_or(is_feeder, is_root))
    def _():
        near_part_copy.wait_send()
        far_part_copy.wait_send()

    @pl.when(depth != 0)
    def _():
        main_copy.wait_send()
        column_copy.wait_send()

    @pl.when(is_root)
    def _():
        forward_copy.wait_send()
        far_forward_copy.wait_send()

        @pl.loop(1, planes)
        def _(step):
            plane_copy(lax.rem(here + step, planes), here).wait_send()

        @pl.loop(1, column)
        def _(z):
            total_copy(z).wait_send()


def body(
    magnetogram,
    col_owner,
    col_offset,
    phi_weight,
    theta_weight,
    radial_coef,
    theta_coef,
    phi_coef,
    start_field,
):
    phis, rows = lax.axis_size("phi"), lax.axis_size("row")
    layers, cells, width = start_field.shape
    planes, column = phis // 2, 2 * rows
    slots = phis * CAP
    tall = cells + 2 * PAD
    deep = layers + 2 * EDGE
    dma = pltpu.SemaphoreType.DMA
    anywhere = pl.BlockSpec(memory_space=pl.ANY)
    operands = (
        magnetogram,
        col_owner.reshape(1, -1),
        col_offset.reshape(1, -1),
        phi_weight.T,
        theta_weight,
        radial_coef,
        theta_coef.reshape(1, -1),
        phi_coef.reshape(-1, width),
        start_field,
    )
    local = [pltpu.VMEM(x.shape, x.dtype) for x in operands[:8]]
    local[5] = pltpu.SMEM(radial_coef.shape, F32)
    fields, coef = pl.pallas_call(
        functools.partial(kernel, phis, rows),
        out_shape=(
            pltpu.VMEM((5,) + start_field.shape, F32),
            pltpu.VMEM((2, width), F32),
        ),
        in_specs=[anywhere] * 9,
        out_specs=(pl.BlockSpec(memory_space=pltpu.VMEM),) * 2,
        scratch_shapes=local
        + [
            pltpu.VMEM((planes, 2 * CAP, width), BF16),
            pltpu.VMEM((planes, 2 * CAP, width), BF16),
            pltpu.VMEM((cells, planes * CAP), BF16),
            pltpu.VMEM((cells, planes * CAP), BF16),
            pltpu.VMEM((2, cells, width), F32),
            pltpu.VMEM((6, 2, cells, width), F32),
            pltpu.VMEM((7, 2, PAD, width), F32),
            pltpu.VMEM((7, PAD, width), F32),
            pltpu.VMEM((2, tall, width), F32),
            pltpu.VMEM((tall, width), F32),
            pltpu.VMEM((PAD, width), F32),
            pltpu.VMEM((deep, cells, width), F32),
            pltpu.VMEM((deep, PAD, width), F32),
            pltpu.VMEM((deep, PAD, width), F32),
            pltpu.VMEM((4, cells, width), F32),
            pltpu.VMEM((4, tall, width), F32),
            pltpu.VMEM((1, deep, tall, width), F32),
            pltpu.VMEM((2, deep, tall, width), F32),
            pltpu.VMEM((2, 2, tall, width), F32),
            pltpu.VMEM((1, 5, deep, tall, width), F32),
            pltpu.VMEM((2, 1, width), F32),
            pltpu.VMEM((column, 1, width), F32),
            pltpu.VMEM((planes, 1, width), F32),
            pltpu.VMEM((1, width), F32),
            dma((9,)),
            dma((planes,)),
            dma((planes,)),
            dma,
            dma,
            dma((3,)),
            dma((6,)),
            dma((7,)),
            dma((7,)),
            dma((2,)),
            dma((2,)),
            dma((3,)),
            dma((3,)),
            dma((3,)),
            dma((3,)),
            dma((3,)),
            dma((3,)),
            dma,
            dma,
            dma,
            dma((column,)),
            dma((planes,)),
            dma((planes,)),
            dma((column,)),
            dma,
        ],
        compiler_params=pltpu.CompilerParams(collective_id=0, has_side_effects=True),
    )(*operands)
    along, across = coef[0], coef[1]
    solution_field = start_field + along * fields[1] - across * fields[3]
    residual = fields[0] - along * fields[2] + across * fields[4]
    return solution_field, residual


def solution(mesh):
    in_specs = (
        P("phi", "row"),
        P("phi"),
        P("phi"),
        P(None, "phi"),
        P("row", None),
        P(),
        P(),
        P(),
        P("row", "phi", None),
    )
    out_specs = (P("row", "phi", None), P("row", "phi", None))
    return jax.shard_map(body, mesh=mesh, in_specs=in_specs, out_specs=out_specs, check_vma=False)
```
